32 devices in a mesh: groups: 2 (over y), seq: 4 (over z), head: 2 (over x), rep: 2 (over core).
Axes of the slice: x: 2, y: 2, z: 4, core: 2. Of those that a mesh axis runs over, the one named last changes fastest.
Arguments:
- query_proj: bfloat16 [2048, 4096], P(('groups', 'seq'), ('head', 'rep')), parts along dimension 0, may hold values from -6 to 6
- key_proj: bfloat16 [2048, 4096], P(('groups', 'seq'), ('head', 'rep')), parts along dimension 0, may hold values from -6 to 6
- value_proj: bfloat16 [2048, 4096], P(('groups', 'seq'), ('head', 'rep')), parts along dimension 0, may hold values from -6 to 6
- forget_logits: bfloat16 [2048, 4096], P(('groups', 'seq'), ('head', 'rep')), parts along dimension 0, may hold values from -8 to 8
- decay_rate: float32 [4096], P(('head', 'rep')), may hold values from 0.001 to 0.1
- beta_logits: bfloat16 [2048, 32], P(('groups', 'seq'), ('head', 'rep')), parts along dimension 0, may hold values from -4.5 to -0.5
- gate_logits: bfloat16 [2048, 4096], P(('groups', 'seq'), ('head', 'rep')), parts along dimension 0, may hold values from -6 to 6
- norm_gain: float32 [128], replicated, may hold values from 0.25 to 1.75
- out_weight: bfloat16 [4096, 2304], P(('head', 'rep')), may hold values from -0.125 to 0.125
- stream_starts: int32 [16], P('groups'), parts along dimension 0, may hold values from 0 to 1023, as said below
- stream_slots: int32 [16], P('groups'), parts along dimension 0, may hold values from 0 to 7, each once
Outputs:
- layer_out: bfloat16 [2048, 2304], P(('groups', 'seq'), ('head', 'rep')), parts along dimension 0
- slot_states: bfloat16 [16, 32, 128, 128], P(('groups', 'seq'), ('head', 'rep')), parts along dimension 0
The draws below stay inside these ranges and needn't reach their ends.
There are 2 independent parts, one for each index of `groups`. The reference program is written for one: setup_inputs(seed, part) draws one part's arguments, and reference() takes and returns one part's arrays. A program takes and returns all parts, laid end to end along the dimension named above; an argument that names none is the same for every part. Nothing has to cross between parts.
Inputs may be any that keep to these rules, and one draw needn't show every extreme that they name: `stream_starts`: strictly increasing, the first is 0; at most 4 streams end within one index of seq's 256 tokens, and in every draw some index has exactly 4 ends. `stream_slots`: each slot once; slot s is kept by index s // 2 of seq.
All inputs are finite; a program needn't handle non-finite values.
Results may differ from the reference program's by a relative error of at most 0.014.
Values may be sent and summed in bfloat16 or wider, within the bound.
A program may use at most 64 MiB of HBM per device.

```python
import math
import jax
import jax.numpy as jnp
from jax import lax

HEAD_TOTAL = 32
KEY_SIZE = 128
DV = 128
D = 2304
TOKEN_PER_PART = 256
STREAMS_DEV = 2
HEAD_GROUPS = 4
HEADS_DEV = 8
TOKEN_TOTAL = 1024
STREAMS = 8


def shared_pair(key):
    first_key, second_key = jax.random.split(jax.random.fold_in(key, 11))
    common_key = jax.random.fold_in(key, 13)
    full_shape = (TOKEN_TOTAL, HEAD_TOTAL * KEY_SIZE)
    opening_sample = jax.random.normal(first_key, full_shape, jnp.float32)
    second_draw = jax.random.normal(second_key, full_shape, jnp.float32)
    common = jax.random.normal(common_key, (HEAD_TOTAL, KEY_SIZE), jnp.float32)
    common_rows = jnp.broadcast_to(common.reshape(1, HEAD_TOTAL * KEY_SIZE), full_shape)
    key_rows = 0.8 * common_rows + 0.6 * opening_sample
    query_rows = 0.6 * key_rows + 0.8 * second_draw
    return (jnp.clip(key_rows, -6.0, 6.0), jnp.clip(query_rows, -6.0, 6.0))


def draw_key_proj(key, part):
    return shared_pair(key)[0].astype(jnp.bfloat16)


def draw_query_proj(key, part):
    return shared_pair(key)[1].astype(jnp.bfloat16)


def draw_forget_logits(key, part):
    root_random_key, offset_random_key, spell_random_key, location_random_key = jax.random.split(jax.random.fold_in(key, 21), 4)
    shards = TOKEN_TOTAL // TOKEN_PER_PART
    opening_sample = -1.0 + 0.7 * jax.random.normal(root_random_key, (TOKEN_TOTAL, HEAD_TOTAL * KEY_SIZE), jnp.float32)
    shifts = jax.random.uniform(offset_random_key, (shards, 1, HEAD_TOTAL * KEY_SIZE), jnp.float32, -0.6, 0.6)
    opening_sample = (opening_sample.reshape(shards, TOKEN_PER_PART, HEAD_TOTAL * KEY_SIZE) + shifts).reshape(TOKEN_TOTAL, HEAD_TOTAL * KEY_SIZE)
    spell_runs = max(2, TOKEN_TOTAL // 2048)
    spell_length = max(2, min(32, TOKEN_PER_PART // 4))
    stream_begins = jax.random.randint(location_random_key, (spell_runs,), 0, TOKEN_TOTAL - spell_length + 1)
    token_positions = jnp.arange(TOKEN_TOTAL)
    within_flags = jnp.any((token_positions[:, None] >= stream_begins[None, :]) & (token_positions[:, None] < stream_begins[None, :] + spell_length), axis=1)
    spell_value_rows = 7.0 + 0.5 * jax.random.uniform(spell_random_key, (TOKEN_TOTAL, HEAD_TOTAL * KEY_SIZE), jnp.float32, -1.0, 1.0)
    return jnp.clip(jnp.where(within_flags[:, None], spell_value_rows, opening_sample), -8.0, 8.0).astype(jnp.bfloat16)


def draw_decay_rate(key, part):
    slow_key = jax.random.fold_in(jax.random.fold_in(key, 41), 1)
    log_rates = jax.random.uniform(slow_key, (HEAD_TOTAL * KEY_SIZE,), jnp.float32, math.log(0.001), math.log(0.1))
    return jnp.clip(jnp.exp(log_rates), 0.001, 0.1).astype(jnp.float32)


def draw_stream_starts(key, part):
    shards = TOKEN_TOTAL // TOKEN_PER_PART
    pair_count = shards // 2
    most_ends = 2 * STREAMS_DEV
    count_key, force_key, location_random_key = jax.random.split(jax.random.fold_in(key, 31), 3)
    firsts = jax.random.randint(count_key, (pair_count,), 0, most_ends + 1)
    pair_ids = jnp.arange(pair_count)
    firsts = jnp.where(pair_ids == pair_count - 1, jnp.minimum(firsts, most_ends - 1), firsts)
    forced = jax.random.randint(force_key, (), 0, pair_count)
    pinned = jnp.where(forced == pair_count - 1, 0, most_ends)
    firsts = jnp.where(pair_ids == forced, pinned, firsts)
    counts = jnp.stack([firsts, most_ends - firsts], axis=1).reshape(shards)
    orders = jax.vmap(lambda sub_key: jax.random.permutation(sub_key, TOKEN_PER_PART))(jax.random.split(location_random_key, shards))
    tail_row = orders[shards - 1]
    last_rank = tail_row[TOKEN_PER_PART - 1]
    token_positions = jnp.arange(TOKEN_PER_PART)
    tail_row = jnp.where(token_positions == TOKEN_PER_PART - 1, -1, jnp.where(tail_row > last_rank, tail_row - 1, tail_row))
    orders = orders.at[shards - 1].set(tail_row)
    limits = counts - (jnp.arange(shards) == shards - 1).astype(counts.dtype)
    ending = (orders < limits[:, None]).reshape(TOKEN_TOTAL)
    rank_of = jnp.cumsum(ending.astype(jnp.int32)) - 1
    targets = jnp.where(ending, rank_of, STREAMS)
    finals = jnp.zeros((STREAMS,), jnp.int32).at[targets].set(jnp.arange(TOKEN_TOTAL, dtype=jnp.int32), mode='drop')
    return jnp.concatenate([jnp.zeros((1,), jnp.int32), finals[:-1] + 1]).astype(jnp.int32)


def strengthened(array, stream_key, source, target, shards_of, factor):
    owner, partner = [(jnp.arange(array.shape[dim]) // (array.shape[dim] // shards_of)).reshape([-1 if axis == dim else 1 for axis in range(array.ndim)]) for dim in (source, target)]
    chosen = jax.random.permutation(stream_key, shards_of)[partner]
    strong = (owner == chosen) | (owner == (partner + shards_of // 2) % shards_of)
    return jnp.where(strong, factor * array, array)


def block_scale(own_key, extent, cuts, low, top_value):
    factor_of, own = 1.0, jax.random.fold_in(own_key, 6)
    for axis_at, parts in cuts:
        steps = jnp.exp(jax.random.uniform(jax.random.fold_in(own, axis_at), (parts,), jnp.float32, low / len(cuts), top_value / len(cuts)))
        factor_of = factor_of * jnp.repeat(steps, extent[axis_at] // parts).reshape([-1 if axis == axis_at else 1 for axis in range(len(extent))])
    return factor_of


def normal_values(stream_key, shape, spread, most, cuts=(), kind=jnp.bfloat16):
    factor_of = block_scale(stream_key, shape, cuts, -0.22, 0.18) if cuts else 1.0
    result = jax.random.normal(stream_key, shape, jnp.float32) * spread * factor_of
    return jnp.minimum(jnp.maximum(result, -most), most).astype(kind)


def gaussian_with(rng, extent, deviation, bound, cuts, heavy, kind=jnp.bfloat16):
    values = deviation * jax.random.normal(rng, extent, jnp.float32)
    if cuts:
        values = values * block_scale(rng, extent, cuts, -0.22, 0.18)
    return jnp.clip(strengthened(values, jax.random.fold_in(rng, 3), *heavy), -bound, bound).astype(kind)


def setup_inputs(seed: int = 0, part: int = 0) -> dict:
    streams_of = jax.random.split(jax.random.key(seed), 12)
    part_splits = jax.random.split(jax.random.fold_in(streams_of[11], part), 12)
    return {
        "query_proj": draw_query_proj(jax.random.fold_in(jax.random.fold_in(streams_of[11], part), 71), part),
        "key_proj": draw_key_proj(jax.random.fold_in(jax.random.fold_in(streams_of[11], part), 71), part),
        "value_proj": normal_values(part_splits[2], (TOKEN_TOTAL, HEAD_TOTAL * DV), 1.0, 6.0, ((0, 4), (1, 4))),
        "forget_logits": draw_forget_logits(jax.random.fold_in(jax.random.fold_in(streams_of[11], part), 71), part),
        "decay_rate": draw_decay_rate(jax.random.fold_in(streams_of[11], 71), part),
        "beta_logits": jnp.clip(-4.5 + 4.0 * jax.random.uniform(part_splits[5], (TOKEN_TOTAL, HEAD_TOTAL), jnp.float32) ** block_scale(part_splits[5], (TOKEN_TOTAL, HEAD_TOTAL), ((0, 4), (1, 4)), -0.2, 0.2), -4.5, -0.5).astype(jnp.bfloat16),
        "gate_logits": normal_values(part_splits[6], (TOKEN_TOTAL, HEAD_TOTAL * DV), 1.0, 6.0, ((0, 4), (1, 4))),
        "norm_gain": jnp.clip(1.0 + 0.15 * jax.random.normal(streams_of[7], (DV,), jnp.float32), 0.25, 1.75),
        "out_weight": gaussian_with(streams_of[8], (HEAD_TOTAL * DV, D), (HEAD_TOTAL * DV) ** -0.5, 0.125, ((0, 4),), (0, 1, 4, 2.0)),
        "stream_starts": draw_stream_starts(jax.random.fold_in(jax.random.fold_in(streams_of[11], part), 71), part),
        "stream_slots": jax.random.permutation(part_splits[10], STREAMS).astype(jnp.int32),
    }


SMALLEST_STEP = lax.Precision.HIGHEST

def unit_rows(rows, row_width):
    shaped = rows.astype(jnp.float32).reshape(rows.shape[0], -1, row_width)
    return shaped * lax.rsqrt(lax.optimization_barrier(jnp.sum(shaped * shaped, axis=-1, keepdims=True)) + 1e-06)

def reference(query_proj, key_proj, value_proj, forget_logits, decay_rate, beta_logits, gate_logits, norm_gain, out_weight, stream_starts, stream_slots):
    token_count = query_proj.shape[0]
    queries = unit_rows(query_proj, KEY_SIZE)
    keys_unit = unit_rows(key_proj, KEY_SIZE)
    values_all = value_proj.astype(jnp.float32).reshape(token_count, HEAD_TOTAL, DV)
    decays = jnp.exp(-decay_rate.reshape(HEAD_TOTAL, KEY_SIZE) * jax.nn.softplus(forget_logits.astype(jnp.float32).reshape(token_count, HEAD_TOTAL, KEY_SIZE)))
    betas = jax.nn.sigmoid(beta_logits.astype(jnp.float32))
    token_index = jnp.arange(token_count, dtype=jnp.int32)
    starting = jnp.any(token_index[:, None] == stream_starts[None, :], axis=1)
    ending = jnp.concatenate([starting[1:], jnp.ones((1,), dtype=bool)])
    stream_of = lax.optimization_barrier(jnp.sum((stream_starts[None, :] <= token_index[:, None]).astype(jnp.int32), axis=1)) - 1
    stream_ids = jnp.arange(STREAMS, dtype=jnp.int32)
    slot_of = lax.optimization_barrier(jnp.sum(jnp.where(stream_of[:, None] == stream_ids[None, :], stream_slots[None, :], 0), axis=1)).astype(jnp.int32)

    def advance(carry, slices):
        memory_state_matrix, slot_store = carry
        single_query_row, single_key_row, value_row, decay_row, beta_row, start_flag, end_flag, slot_index = slices
        memory_state_matrix = jnp.where(start_flag, jnp.zeros_like(memory_state_matrix), memory_state_matrix)
        memory_state_matrix = decay_row[:, :, None] * memory_state_matrix
        recalled_values = jnp.einsum('is,isq->iq', single_key_row, memory_state_matrix, precision=SMALLEST_STEP)
        memory_state_matrix = memory_state_matrix + beta_row[:, None, None] * single_key_row[:, :, None] * (value_row - recalled_values)[:, None, :]
        readout_row = jnp.einsum('is,isq->iq', single_query_row, memory_state_matrix, precision=SMALLEST_STEP)
        previous = lax.dynamic_index_in_dim(slot_store, slot_index, 0, keepdims=False)
        slot_store = lax.dynamic_update_index_in_dim(slot_store, jnp.where(end_flag, memory_state_matrix, previous), slot_index, 0)
        return ((memory_state_matrix, slot_store), readout_row)
    initial = (jnp.zeros((HEAD_TOTAL, KEY_SIZE, DV), jnp.float32), jnp.zeros((STREAMS, HEAD_TOTAL, KEY_SIZE, DV), jnp.float32))
    final_carry, read_out = lax.scan(advance, initial, (queries, keys_unit, values_all, decays, betas, starting, ending, slot_of))
    inverse_rms = lax.rsqrt(lax.optimization_barrier(jnp.mean(read_out * read_out, axis=-1, keepdims=True)) + 1e-05)
    gates = jax.nn.sigmoid(gate_logits.astype(jnp.float32).reshape(token_count, HEAD_TOTAL, DV))
    hidden = (read_out * inverse_rms * norm_gain * gates).reshape(token_count, HEAD_TOTAL * DV).astype(jnp.bfloat16)
    group_width = HEADS_DEV * DV
    summed = jnp.zeros((token_count, D), jnp.float32)
    for group_index in range(HEAD_GROUPS):
        lower_col = group_index * group_width
        partial_value = jnp.dot(hidden[:, lower_col:lower_col + group_width], out_weight[lower_col:lower_col + group_width], preferred_element_type=jnp.float32)
        rounded = lax.optimization_barrier(partial_value.astype(jnp.bfloat16))
        summed = summed + rounded.astype(jnp.float32)
    return (summed.astype(jnp.bfloat16), final_carry[1].astype(jnp.bfloat16))
```

```python
import functools
import jax
import jax.numpy as jnp
from jax import lax
from jax.experimental import pallas as pl
from jax.experimental.pallas import tpu as pltpu
from jax.sharding import PartitionSpec as P

ENDS_MAX = 4
PAIR = 2
BASE = 16
F32 = jnp.float32
BF16 = jnp.bfloat16
I32 = jnp.int32
NN = (((1,), (0,)), ((), ()))
NT = (((1,), (1,)), ((), ()))


def halves(x):
    high = x.astype(BF16)
    return high, (x - high.astype(F32)).astype(BF16)


def dot(a, b, dims=NN):
    return lax.dot_general(a, b, dims, preferred_element_type=F32)


def wide(x):
    return jnp.concatenate(halves(x), axis=1)


def twice(x, axis):
    return jnp.concatenate([x, x], axis=axis)


def mm4(a, b):
    both = dot(a, twice(b, 0))
    half = both.shape[1] // 2
    return both[:, :half] + both[:, half:]


def unit(x):
    return x * lax.rsqrt(jnp.sum(x * x, axis=-1, keepdims=True) + 1e-06)


def block_inverses(mats, level):
    size = mats[0].shape[0]
    row = lax.broadcasted_iota(I32, (size, size), 0)
    col = lax.broadcasted_iota(I32, (size, size), 1)
    eye = (row == col).astype(F32)
    powers = [jnp.where(level == 0.0, m, 0.0) for m in mats]
    result = [eye - p for p in powers]
    splits = [wide(p) for p in powers]
    powers = [mm4(s, s) for s in splits]
    width = 4
    while width < BASE:
        splits = [wide(p) for p in powers]
        both = [mm4(jnp.concatenate([wide(r), s], axis=0), s) for r, s in zip(result, splits)]
        result = [r + b[:size] for r, b in zip(result, both)]
        powers = [b[size:] for b in both]
        width *= 2
    splits = [wide(p) for p in powers]
    result = [r + mm4(wide(r), s) for r, s in zip(result, splits)]
    width = BASE
    step = 1
    while width < size:
        splits = [wide(r) for r in result]
        mids = [mm4(wide(jnp.where(level == float(step), m, 0.0)), s) for m, s in zip(mats, splits)]
        result = [r - mm4(s, wide(t)) for r, s, t in zip(result, splits, mids)]
        width *= 2
        step += 1
    return result


def fused_kernel(n, nh, lanes, *refs):
    (starts_ref, slots_ref, q_hbm, k_hbm, v_hbm, f_hbm, rate_hbm, beta_hbm, gate_hbm, gain_hbm, weight_hbm,
     layer_ref, slot_ref,
     qv, kv, vv, fv, gate, rate, beta_raw, gain, weight,
     sums, strict, lower, level, first, masks, betas, table,
     local, mapcorr, tail, own, moved, hidden, state_in, state_out,
     up_in, up_out, dn_in, dn_out, parts, pair_in, sums_out, cross_in,
     load_sem, misc_sem,
     st_send, st_recv, up_send, up_recv, dn_send, dn_recv, p_send, p_recv, c_send, c_recv) = refs
    length, total = qv.shape
    heads = own.shape[0]
    owned = own.shape[1]
    width = total // heads
    half = length // 2
    pairs = heads // PAIR
    streams = starts_ref.shape[0]
    piece = layer_ref.shape[1]
    me = lax.axis_index("seq")
    head_at = lax.axis_index("head")
    rep_at = lax.axis_index("rep")
    mesh_id = pl.DeviceIdType.MESH
    up, down, partner = {"seq": me + 1}, {"seq": me - 1}, {"rep": 1 - rep_at}
    has_up, has_down = me < n - 1, me > 0
    inner = has_up & has_down

    def pair_load(p, i):
        src, dst = ((f_hbm, fv), (k_hbm, kv), (q_hbm, qv), (v_hbm, vv))[i]
        cols = pl.ds(pl.multiple_of(p * PAIR * width, width), PAIR * width)
        return pltpu.make_async_copy(src.at[:, cols], dst.at[:, cols], load_sem.at[p, i])

    small = [pltpu.make_async_copy(src, dst, misc_sem.at[i]) for i, (src, dst) in enumerate(
        ((beta_hbm, beta_raw), (rate_hbm, rate), (gain_hbm, gain), (gate_hbm, gate), (weight_hbm, weight)))]
    for copy in small[:3]:
        copy.start()
    for p in range(pairs):
        for i in range(4):
            pair_load(p, i).start()
    for copy in small[3:]:
        copy.start()

    barrier = pltpu.get_barrier_semaphore()

    @pl.when(has_up)
    def _():
        pl.semaphore_signal(barrier, inc=1, device_id=up, device_id_type=mesh_id)

    @pl.when(has_down)
    def _():
        pl.semaphore_signal(barrier, inc=1, device_id=down, device_id_type=mesh_id)

    pl.semaphore_signal(barrier, inc=1, device_id=partner, device_id_type=mesh_id)
    for j in range(1, nh):
        pl.semaphore_signal(barrier, inc=1, device_id={"head": lax.rem(head_at + j, nh)}, device_id_type=mesh_id)

    def remote(src, dst, send, recv, target):
        return pltpu.make_async_remote_copy(src_ref=src, dst_ref=dst, send_sem=send, recv_sem=recv,
                                            device_id=target, device_id_type=mesh_id)

    def state_copy(h):
        return remote(state_out.at[h], state_in.at[h], st_send.at[h], st_recv.at[h], up)

    def up_copy(h):
        return remote(up_out.at[h], up_in.at[h], up_send.at[h], up_recv.at[h], up)

    def dn_copy(h):
        return remote(dn_out.at[h], dn_in.at[h], dn_send.at[h], dn_recv.at[h], down)

    def pair_copy(j):
        return remote(parts.at[2 * j + 1 - rep_at], pair_in.at[j], p_send.at[j], p_recv.at[j], partner)

    def cross_copy(j):
        return remote(sums_out.at[j], cross_in.at[j], c_send.at[j], c_recv.at[j],
                      {"head": lax.rem(head_at + j, nh)})

    anchor = me * length
    begins = [starts_ref[j] for j in range(streams)]
    slots = [slots_ref[j] for j in range(streams)]
    ends = begins[1:] + [n * length]
    count = lambda flags: sum(f.astype(I32) for f in flags)
    where = jnp.where
    end_at = [count([e > p * length for p in range(1, n)]) if isinstance(e, jax.Array) else jnp.int32(n - 1)
              for e in ends]
    dest = [count([s >= p * owned for p in range(1, n)]) for s in slots]
    here = [e == me for e in end_at]
    before = where(me == 0, -1, count([b <= anchor - 1 for b in begins]))
    open_id = 1 + count([e <= me for e in end_at])
    open_flag = 1.0 - where(count(here) > 0, 1.0, 0.0)

    def colours(order, crossing, free):
        busy = [None] * lanes
        result = [None] * streams
        for j in order:
            left = crossing(j)
            pick_at = jnp.int32(-1)
            for c in range(lanes):
                pick = left if busy[c] is None else left & free(busy[c], end_at[j])
                pick_at = where(pick, c, pick_at)
                busy[c] = where(pick, dest[j], jnp.int32(0) if order[0] == 0 else jnp.int32(n)) if busy[c] is None \
                    else where(pick, dest[j], busy[c])
                left = left & jnp.logical_not(pick)
            result[j] = pick_at
        return result

    up_lane = colours(list(range(streams)), lambda j: dest[j] > end_at[j], lambda b, e: b <= e)
    dn_lane = colours(list(range(streams))[::-1], lambda j: dest[j] < end_at[j], lambda b, e: b >= e)
    code = []
    for j in range(streams):
        home = where(dest[j] == me, slots[j] - me * owned + 1, 0)
        rise = where(up_lane[j] >= 0, up_lane[j] + 1 + owned, 0)
        fall = where(dn_lane[j] >= 0, dn_lane[j] + 1 + owned + lanes, 0)
        code.append(where(here[j], home + rise + fall, 0))
    begun = sum(where(before == j + 1, code[j], 0) for j in range(streams))
    entries = owned + 2 * lanes
    for e in range(entries):
        table[e] = where(begun == e + 1, 1.0, 0.0)
    at = entries
    for lane_of, between in ((up_lane, lambda j: (end_at[j] < me) & (dest[j] > me)),
                             (dn_lane, lambda j: (end_at[j] > me) & (dest[j] < me))):
        passing = [where(between(j), lane_of[j], -1) for j in range(streams)]
        away = [jnp.logical_not(here[j]) & (dest[j] == me) for j in range(streams)]
        landing = [[where(away[j] & (slots[j] == me * owned + k), lane_of[j], -1) for j in range(streams)]
                   for k in range(owned)]
        for c in range(lanes):
            table[at] = where(count([x == c for x in passing]) > 0, 1.0, 0.0)
            for k in range(owned):
                table[at + 1 + k] = where(count([x == c for x in landing[k]]) > 0, 1.0, 0.0)
            at += 1 + owned
    up_base, dn_base = entries, entries + lanes * (1 + owned)

    pos_row = lax.broadcasted_iota(I32, (16, length), 1) + anchor
    pos_col = lax.broadcasted_iota(I32, (length, width), 0) + anchor
    seg_row = jnp.zeros((16, length), I32)
    seg_col = jnp.zeros((length, width), I32)
    for j in range(streams):
        seg_row = seg_row + where(pos_row >= begins[j], 1, 0)
        seg_col = seg_col + where(pos_col >= begins[j], 1, 0)
    code_row = jnp.zeros((16, length), I32)
    for j in range(streams):
        code_row = where(seg_row == j + 1, code[j], code_row)
    for e in range(entries):
        masks[e] = where(code_row == e + 1, 1.0, 0.0).astype(BF16)
    masks[entries] = where(seg_row == open_id, 1.0, 0.0).astype(BF16)
    first_row = where(seg_row == before, 1.0, 0.0)
    masks[entries + 1] = first_row.astype(BF16)
    any_first = jnp.max(first_row[:1])
    first[...] = where(seg_col == before, 1.0, 0.0)
    row = lax.broadcasted_iota(I32, (length, length), 0)
    col = lax.broadcasted_iota(I32, (length, length), 1)
    same = jnp.concatenate([seg_col] * (length // width), axis=1) == seg_row[:1]
    sums[:length] = where(row >= col, 1.0, 0.0).astype(BF16)
    sums[length:] = where(same & (col > row), 1.0, 0.0).astype(BF16)
    strict[...] = where(same & (row > col), 1.0, 0.0)
    lower[...] = where(same & (row >= col), 1.0, 0.0)
    hrow, hcol = row[:half, :half], col[:half, :half]
    depth = jnp.zeros((half, half), F32)
    size = BASE
    while size < half:
        depth = depth + where(hrow // size != hcol // size, 1.0, 0.0)
        size *= 2
    level[...] = depth

    small[0].wait()
    betas[...] = jax.nn.sigmoid(beta_raw[...].astype(F32))
    small[1].wait()

    @pl.when(me == 0)
    def _():
        for h in range(heads):
            state_in[h] = jnp.zeros((width, width), BF16)
            up_in[h] = jnp.zeros((lanes, width, width), BF16)

    @pl.when(me == n - 1)
    def _():
        for h in range(heads):
            dn_in[h] = jnp.zeros((lanes, width, width), BF16)

    @pl.when(inner)
    def _():
        pl.semaphore_wait(barrier, nh + 2)

    @pl.when(jnp.logical_not(inner))
    def _():
        pl.semaphore_wait(barrier, nh + 1)

    def local_pair(p):
        for i in range(4):
            pair_load(p, i).wait()
        mats = []
        kept = []
        for i in range(PAIR):
            h = p * PAIR + i
            cols = pl.ds(pl.multiple_of(h * width, width), width)
            q = unit(qv[:, cols].astype(F32))
            k = unit(kv[:, cols].astype(F32))
            x = fv[:, cols].astype(F32)
            soft = jnp.maximum(x, 0.0) + jnp.log(1.0 + jnp.exp(-jnp.abs(x)))
            decay = -(rate[:, cols] * soft)
            summed = dot(sums[...], wide(decay))
            summed = summed[:, :width] + summed[:, width:]
            cum = summed[:length]
            suffix = jnp.exp(summed[length:])
            decayed = jnp.exp(cum) * first[...]
            beta = betas[pl.ds(h, 1), :]
            cum0, cum1 = cum[:half], cum[half:]
            k0, k1, q0, q1 = k[:half], k[half:], q[:half], q[half:]
            mid0 = 0.5 * (cum0[:1] + cum0[-1:])
            mid1 = 0.5 * (cum1[:1] + cum1[-1:])
            up0, up1 = jnp.exp(cum0 - mid0), jnp.exp(cum1 - mid1)
            low0 = (k0 * jnp.exp(mid0 - cum0)).astype(BF16)
            low1 = jnp.concatenate([k0 * jnp.exp(mid1 - cum0), k1 * jnp.exp(mid1 - cum1)], axis=0).astype(BF16)
            block0 = dot(wide(jnp.concatenate([k0 * up0, q0 * up0], axis=0)), twice(low0, 1), NT)
            block1 = dot(wide(jnp.concatenate([k1 * up1, q1 * up1], axis=0)), twice(low1, 1), NT)
            beta0, beta1 = beta[:, :half], beta[:, half:]
            mats.append(where(strict[:half, :half] > 0.0, block0[:half], 0.0) * beta0)
            mats.append(where(strict[half:, half:] > 0.0, block1[:half, half:], 0.0) * beta1)
            link = where(strict[half:, :half] > 0.0, block1[:half, :half], 0.0) * beta0
            reading0 = where(lower[:half, :half] > 0.0, block0[half:], 0.0) * beta0
            reading1 = where(lower[half:, :] > 0.0, block1[half:], 0.0) * beta
            reading = jnp.concatenate([jnp.concatenate([reading0, jnp.zeros_like(reading0)], axis=1), reading1],
                                      axis=0).astype(BF16)
            right = jnp.concatenate([vv[:, cols], (k * decayed).astype(BF16)], axis=1)
            keep = jnp.exp(jnp.sum(first[...] * decay, axis=0, keepdims=True)) * any_first
            ended = ((k * suffix).T * beta).astype(BF16)
            kept.append((wide(link), reading, right, q * decayed, ended, keep))
        inverses = block_inverses(mats, level[...])
        hr = lax.broadcasted_iota(I32, (width, width), 0)
        hc = lax.broadcasted_iota(I32, (width, width), 1)
        for i in range(PAIR):
            h = p * PAIR + i
            link, reading, right, query, ended, keep = kept[i]
            u0 = dot(wide(inverses[2 * i]), twice(right[:half], 0)).astype(BF16)
            rest = right[half:].astype(F32) - dot(link, twice(u0, 0))
            u1 = dot(wide(inverses[2 * i + 1]), twice(rest.astype(BF16), 0)).astype(BF16)
            u = jnp.concatenate([u0, u1], axis=0)
            read = dot(reading, u)
            local[h] = read[:, :width]
            mapcorr[h, width:] = (query - read[:, width:]).astype(BF16)
            chunks = ended.reshape(width // 16, 16, length)
            pick = lambda e: (chunks * masks[e][None]).reshape(width, length)
            states = dot(jnp.concatenate([pick(e) for e in range(entries + 1)], axis=0), u[:, :width])
            for c in range(owned):
                own[h, c] = states[c * width:(c + 1) * width].astype(BF16)
            for c in range(lanes):
                e = owned + c
                up_out[h, c] = states[e * width:(e + 1) * width].astype(BF16)
                e = owned + lanes + c
                dn_out[h, c] = states[e * width:(e + 1) * width].astype(BF16)
            tail[h] = states[entries * width:]
            through = dot(pick(entries + 1), u[:, width:])
            mapcorr[h, :width] = (where(hr == hc, keep, 0.0) - through).astype(BF16)

    def relay(h):
        @pl.when(has_down)
        def _():
            state_copy(h).wait_recv()

        applied = dot(mapcorr[h], state_in[h])
        state_out[h] = (tail[h] + open_flag * applied[:width]).astype(BF16)

        @pl.when(has_up)
        def _():
            state_copy(h).start()

        moved[h] = applied[:width].astype(BF16)
        out = local[h] + applied[width:]
        cols = pl.ds(pl.multiple_of(h * width, width), width)
        scale = lax.rsqrt(jnp.mean(out * out, axis=-1, keepdims=True) + 1e-05)
        hidden[:, cols] = (out * scale * gain[...] * jax.nn.sigmoid(gate[:, cols].astype(F32))).astype(BF16)

    def flow(h, out_buf, in_buf, copy, has_in, has_out, first_entry, base):
        @pl.when(has_in)
        def _():
            copy(h).wait_recv()

        @pl.when(has_in & has_out)
        def _():
            shift = moved[h].astype(F32)
            for c in range(lanes):
                out_buf[h, c] = (out_buf[h, c].astype(F32) + table[first_entry + c] * shift
                                 + table[base + c * (1 + owned)] * in_buf[h, c].astype(F32)).astype(BF16)

        @pl.when(jnp.logical_not(has_in) & has_down)
        def _():
            shift = moved[h].astype(F32)
            for c in range(lanes):
                out_buf[h, c] = (out_buf[h, c].astype(F32) + table[first_entry + c] * shift).astype(BF16)

        @pl.when(has_out)
        def _():
            copy(h).start()

    def settle(h):
        shift = moved[h].astype(F32)
        for k in range(owned):
            value = own[h, k].astype(F32) + table[k] * shift
            for c in range(lanes):
                value = value + table[up_base + c * (1 + owned) + 1 + k] * up_in[h, c].astype(F32)
                value = value + table[dn_base + c * (1 + owned) + 1 + k] * dn_in[h, c].astype(F32)
            slot_ref[k, h] = value.astype(BF16)

    up_lag = 2 * me
    dn_lag = n - 1 + 2 * (n - 1 - me)
    end_lag = jnp.maximum(up_lag, dn_lag)

    def exchange(t, carry):
        hu, hd, hf = t - up_lag, t - dn_lag, t - end_lag

        @pl.when((hu >= 0) & (hu < heads))
        def _():
            flow(hu, up_out, up_in, up_copy, has_down, has_up, owned, up_base)

        @pl.when((hd >= 0) & (hd < heads))
        def _():
            flow(hd, dn_out, dn_in, dn_copy, has_up, has_down, owned + lanes, dn_base)

        @pl.when((hf >= 0) & (hf < heads))
        def _():
            settle(hf)

        return carry

    small[2].wait()
    small[3].wait()

    def advance(t, carry):
        @pl.when(t < pairs)
        def _():
            local_pair(t)

        p = t - me

        @pl.when((p >= 0) & (p < pairs))
        def _():
            for i in range(PAIR):
                relay(p * PAIR + i)

        return exchange(t, carry)

    ticks = pairs + n - 1
    lax.fori_loop(0, ticks, advance, 0)
    small[4].wait()
    if (2 * piece) % 128 == 0:
        for j in range(nh - 1, -1, -1):
            to = lax.rem(head_at + j, nh)
            cols = pl.ds(pl.multiple_of(to * 2 * piece, 128), 2 * piece)
            full = dot(hidden[...], weight[:, cols])
            parts[2 * to] = full[:, :piece].astype(BF16)
            parts[2 * to + 1] = full[:, piece:].astype(BF16)
            pair_copy(to).start()
    else:
        full = dot(hidden[...], weight[...])
        for d in range(2 * nh):
            parts[d] = full[:, d * piece:(d + 1) * piece].astype(BF16)
        for j in range(nh):
            pair_copy(j).start()
    for j in range(nh - 1, 0, -1):
        to = lax.rem(head_at + j, nh)
        pair_copy(to).wait_recv()
        sums_out[j] = (parts[2 * to + rep_at].astype(F32) + pair_in[to].astype(F32)).astype(BF16)
        cross_copy(j).start()
    pair_copy(head_at).wait_recv()
    lax.fori_loop(ticks, heads + 3 * (n - 1), exchange, 0)
    result = parts[2 * head_at + rep_at].astype(F32) + pair_in[head_at].astype(F32)
    for j in range(1, nh):
        cross_copy(j).wait_recv()
        result = result + cross_in[j].astype(F32)
    layer_ref[...] = result.astype(BF16)

    for j in range(nh):
        pair_copy(j).wait_send()
    for j in range(1, nh):
        cross_copy(j).wait_send()

    def drain(h, carry):
        @pl.when(has_up)
        def _():
            state_copy(h).wait_send()
            up_copy(h).wait_send()

        @pl.when(has_down)
        def _():
            dn_copy(h).wait_send()

        return carry

    lax.fori_loop(0, heads, drain, 0)


def fused(starts, slots, q, k, v, f, rate, beta, gates, gain, weight):
    n = lax.axis_size("seq")
    nh = lax.axis_size("head")
    length, total = q.shape
    heads = beta.shape[1]
    width = total // heads
    half = length // 2
    depth, model = weight.shape
    piece = model // (2 * nh)
    owned = slots.shape[0] // n
    lanes = max(min(ENDS_MAX * (p + 1), owned * (n - 1 - p)) for p in range(n - 1))
    entries = owned + 2 * lanes
    vmem = pl.BlockSpec(memory_space=pltpu.VMEM)
    smem = pl.BlockSpec(memory_space=pltpu.SMEM)
    hbm = pl.BlockSpec(memory_space=pl.ANY)
    dma = pltpu.SemaphoreType.DMA
    cube = pltpu.VMEM((heads, width, width), BF16)
    flow = pltpu.VMEM((heads, lanes, width, width), BF16)
    slab = pltpu.VMEM((length, total), BF16)
    return pl.pallas_call(
        functools.partial(fused_kernel, n, nh, lanes),
        out_shape=(jax.ShapeDtypeStruct((length, piece), BF16),
                   jax.ShapeDtypeStruct((owned, heads, width, width), BF16)),
        in_specs=[smem, smem] + [hbm] * 9,
        out_specs=(vmem, vmem),
        scratch_shapes=[
            slab, slab, slab, slab, slab,
            pltpu.VMEM((1, total), F32),
            pltpu.VMEM((heads, length), BF16),
            pltpu.VMEM((1, width), F32),
            pltpu.VMEM((depth, model), BF16),
            pltpu.VMEM((2 * length, length), BF16),
            pltpu.VMEM((length, length), F32),
            pltpu.VMEM((length, length), F32),
            pltpu.VMEM((half, half), F32),
            pltpu.VMEM((length, width), F32),
            pltpu.VMEM((entries + 2, 16, length), BF16),
            pltpu.VMEM((heads, length), F32),
            pltpu.SMEM((entries + 2 * lanes * (1 + owned),), F32),
            pltpu.VMEM((heads, length, width), F32),
            pltpu.VMEM((heads, width + length, width), BF16),
            pltpu.VMEM((heads, width, width), F32),
            pltpu.VMEM((heads, owned, width, width), BF16),
            cube,
            slab,
            cube, cube,
            flow, flow, flow, flow,
            pltpu.VMEM((2 * nh, length, piece), BF16),
            pltpu.VMEM((nh, length, piece), BF16),
            pltpu.VMEM((nh, length, piece), BF16),
            pltpu.VMEM((nh, length, piece), BF16),
            dma((heads // PAIR, 4)), dma((5,)),
            dma((heads,)), dma((heads,)), dma((heads,)), dma((heads,)), dma((heads,)), dma((heads,)),
            dma((nh,)), dma((nh,)), dma((nh,)), dma((nh,)),
        ],
        compiler_params=pltpu.CompilerParams(collective_id=0, has_side_effects=True,
                                             vmem_limit_bytes=60 << 20),
        name="fused",
    )(starts, slots, q, k, v, f, rate.reshape(1, -1), beta.T, gates, gain.reshape(1, -1), weight)


def per_device(query_proj, key_proj, value_proj, forget_logits, decay_rate, beta_logits,
               gate_logits, norm_gain, out_weight, stream_starts, stream_slots):
    return fused(stream_starts, stream_slots, query_proj, key_proj, value_proj, forget_logits, decay_rate,
                 beta_logits, gate_logits, norm_gain, out_weight)


def solution(mesh):
    rows = P(("groups", "seq"), ("head", "rep"))
    in_specs = (rows, rows, rows, rows, P(("head", "rep")), rows, rows, P(),
                P(("head", "rep"), None), P("groups"), P("groups"))
    out_specs = (rows, P(("groups", "seq"), ("head", "rep"), None, None))
    return jax.shard_map(per_device, mesh=mesh, in_specs=in_specs, out_specs=out_specs, check_vma=False)
```

```python
import functools
import jax
import jax.numpy as jnp
from jax import lax
from jax.experimental import pallas as pl
from jax.experimental.pallas import tpu as pltpu
from jax.sharding import PartitionSpec as P

ENDS_MAX = 4
PAIR = 2
BASE = 16
F32 = jnp.float32
BF16 = jnp.bfloat16
I32 = jnp.int32
NN = (((1,), (0,)), ((), ()))
NT = (((1,), (1,)), ((), ()))


def halves(x):
    high = x.astype(BF16)
    return high, (x - high.astype(F32)).astype(BF16)


def dot(a, b, dims=NN):
    return lax.dot_general(a, b, dims, preferred_element_type=F32)


def wide(x):
    return jnp.concatenate(halves(x), axis=1)


def twice(x, axis):
    return jnp.concatenate([x, x], axis=axis)


def mm4(a, b):
    both = dot(a, twice(b, 0))
    half = both.shape[1] // 2
    return both[:, :half] + both[:, half:]


def unit(x):
    return x * lax.rsqrt(jnp.sum(x * x, axis=-1, keepdims=True) + 1e-06)


def block_inverses(mats, level):
    size = mats[0].shape[0]
    row = lax.broadcasted_iota(I32, (size, size), 0)
    col = lax.broadcasted_iota(I32, (size, size), 1)
    eye = (row == col).astype(F32)
    powers = [jnp.where(level == 0.0, m, 0.0) for m in mats]
    result = [eye - p for p in powers]
    splits = [wide(p) for p in powers]
    powers = [mm4(s, s) for s in splits]
    yield None
    width = 4
    while width < BASE:
        splits = [wide(p) for p in powers]
        both = [mm4(jnp.concatenate([wide(r), s], axis=0), s) for r, s in zip(result, splits)]
        result = [r + b[:size] for r, b in zip(result, both)]
        powers = [b[size:] for b in both]
        width *= 2
        yield None
    splits = [wide(p) for p in powers]
    result = [r + mm4(wide(r), s) for r, s in zip(result, splits)]
    yield None
    width = BASE
    step = 1
    while width < size:
        splits = [wide(r) for r in result]
        mids = [mm4(wide(jnp.where(level == float(step), m, 0.0)), s) for m, s in zip(mats, splits)]
        yield None
        result = [r - mm4(s, wide(t)) for r, s, t in zip(result, splits, mids)]
        width *= 2
        step += 1
        yield None
    yield result


def fused_kernel(n, nh, lanes, *refs):
    (starts_ref, slots_ref, q_hbm, k_hbm, v_hbm, f_hbm, rate_hbm, beta_hbm, gate_hbm, gain_hbm, weight_hbm,
     layer_ref, slot_ref,
     qv, kv, vv, fv, gate, rate, beta_raw, gain, weight,
     sums, strict, lower, level, first, masks, betas, table,
     mat_s, link_s, reading_s, right_s, query_s, ended_s, keep_s,
     local, mapcorr, tail, own, moved, hidden, state_in, state_out,
     up_in, up_out, dn_in, dn_out, parts, pair_in, sums_out, cross_in,
     load_sem, misc_sem,
     st_send, st_recv, up_send, up_recv, dn_send, dn_recv, p_send, p_recv, c_send, c_recv) = refs
    length, total = qv.shape
    heads = own.shape[0]
    owned = own.shape[1]
    width = total // heads
    half = length // 2
    pairs = heads // PAIR
    streams = starts_ref.shape[0]
    piece = layer_ref.shape[0]
    me = lax.axis_index("seq")
    head_at = lax.axis_index("head")
    rep_at = lax.axis_index("rep")
    mesh_id = pl.DeviceIdType.MESH
    up, down, partner = {"seq": me + 1}, {"seq": me - 1}, {"rep": 1 - rep_at}
    has_up, has_down = me < n - 1, me > 0
    inner = has_up & has_down

    def pair_load(p, i):
        src, dst = ((f_hbm, fv), (k_hbm, kv), (q_hbm, qv), (v_hbm, vv))[i]
        cols = pl.ds(pl.multiple_of(p * PAIR * width, width), PAIR * width)
        return pltpu.make_async_copy(src.at[:, cols], dst.at[:, cols], load_sem.at[p, i])

    small = [pltpu.make_async_copy(src, dst, misc_sem.at[i]) for i, (src, dst) in enumerate(
        ((beta_hbm, beta_raw), (rate_hbm, rate), (gain_hbm, gain), (gate_hbm, gate), (weight_hbm, weight)))]
    for copy in small[:3]:
        copy.start()
    for p in range(pairs):
        for i in range(4):
            pair_load(p, i).start()
    for copy in small[3:]:
        copy.start()

    barrier = pltpu.get_barrier_semaphore()

    @pl.when(has_up)
    def _():
        pl.semaphore_signal(barrier, inc=1, device_id=up, device_id_type=mesh_id)

    @pl.when(has_down)
    def _():
        pl.semaphore_signal(barrier, inc=1, device_id=down, device_id_type=mesh_id)

    pl.semaphore_signal(barrier, inc=1, device_id=partner, device_id_type=mesh_id)
    for j in range(1, nh):
        pl.semaphore_signal(barrier, inc=1, device_id={"head": lax.rem(head_at + j, nh)}, device_id_type=mesh_id)

    def remote(src, dst, send, recv, target):
        return pltpu.make_async_remote_copy(src_ref=src, dst_ref=dst, send_sem=send, recv_sem=recv,
                                            device_id=target, device_id_type=mesh_id)

    def state_copy(h):
        return remote(state_out.at[h], state_in.at[h], st_send, st_recv.at[h], up)

    def up_copy(h, c):
        return remote(up_out.at[h, c], up_in.at[h, c], up_send, up_recv.at[h, c], up)

    def dn_copy(h, c):
        return remote(dn_out.at[h, c], dn_in.at[h, c], dn_send, dn_recv.at[h, c], down)

    def pair_copy(j):
        return remote(parts.at[2 * j + 1 - rep_at], pair_in.at[j], p_send.at[j], p_recv.at[j], partner)

    def cross_copy(j):
        return remote(sums_out.at[j], cross_in.at[j], c_send.at[j], c_recv.at[j],
                      {"head": lax.rem(head_at + j, nh)})

    anchor = me * length
    begins = [starts_ref[j] for j in range(streams)]
    slots = [slots_ref[j] for j in range(streams)]
    ends = begins[1:] + [n * length]
    count = lambda flags: sum(f.astype(I32) for f in flags)
    where = jnp.where
    end_at = [count([e > p * length for p in range(1, n)]) if isinstance(e, jax.Array) else jnp.int32(n - 1)
              for e in ends]
    dest = [count([s >= p * owned for p in range(1, n)]) for s in slots]
    here = [e == me for e in end_at]
    before = where(me == 0, -1, count([b <= anchor - 1 for b in begins]))
    open_id = 1 + count([e <= me for e in end_at])
    open_flag = 1.0 - where(count(here) > 0, 1.0, 0.0)

    def colours(order, crossing, free, idle, late):
        busy = [jnp.int32(idle)] * lanes
        result = [None] * streams
        for j in order:
            left = crossing(j)
            last = left & late(j)
            left = left & jnp.logical_not(last)
            pick_at = where(last, lanes - 1, -1)
            for c in range(lanes):
                pick = left & free(busy[c], end_at[j])
                pick_at = where(pick, c, pick_at)
                left = left & jnp.logical_not(pick)
                if c == lanes - 1:
                    pick = pick | last
                busy[c] = where(pick, dest[j], busy[c])
            result[j] = pick_at
        return result

    up_lane = colours(list(range(streams)), lambda j: dest[j] > end_at[j], lambda b, e: b <= e, 0,
                      lambda j: jnp.bool_(False))
    dn_lane = colours(list(range(streams))[::-1], lambda j: dest[j] < end_at[j], lambda b, e: b >= e, n,
                      lambda j: (end_at[j] == n - 1) & (begins[j] < (n - 1) * length))
    code = []
    for j in range(streams):
        home = where(dest[j] == me, slots[j] - me * owned + 1, 0)
        rise = where(me == n - 2, slots[j] - (n - 1) * owned, up_lane[j]) + 1 + owned
        rise = where(dest[j] > me, rise, 0)
        fall = where(me == 1, slots[j], dn_lane[j]) + 1 + owned + lanes
        fall = where(dest[j] < me, fall, 0)
        code.append(where(here[j], home + rise + fall, 0))
    begun = sum(where(before == j + 1, code[j], 0) for j in range(streams))
    entries = owned + 2 * lanes
    for e in range(entries):
        table[e] = where(begun == e + 1, 1.0, 0.0)
    at = entries
    span = 1 + 2 * owned
    for lane_of, came, goes, far in ((up_lane, lambda j: end_at[j] < me, lambda j: dest[j] > me, n - 1),
                                     (dn_lane, lambda j: end_at[j] > me, lambda j: dest[j] < me, 0)):
        lane_in = [where(came(j), lane_of[j], -1) for j in range(streams)]
        passing = [where(goes(j), lane_in[j], -1) for j in range(streams)]
        places = [passing] + [[where(slots[j] == at_slot, lane_in[j], -1) for j in range(streams)]
                              for at_slot in [me * owned + k for k in range(owned)] + [far * owned + k for k in range(owned)]]
        for c in range(lanes):
            for x, lane_list in enumerate(places):
                table[at + x] = where(count([y == c for y in lane_list]) > 0, 1.0, 0.0)
            at += span
    up_base, dn_base = entries, entries + lanes * span

    pos_row = lax.broadcasted_iota(I32, (16, length), 1) + anchor
    pos_col = lax.broadcasted_iota(I32, (length, width), 0) + anchor
    seg_row = jnp.zeros((16, length), I32)
    seg_col = jnp.zeros((length, width), I32)
    for j in range(streams):
        seg_row = seg_row + where(pos_row >= begins[j], 1, 0)
        seg_col = seg_col + where(pos_col >= begins[j], 1, 0)
    code_row = jnp.zeros((16, length), I32)
    for j in range(streams):
        code_row = where(seg_row == j + 1, code[j], code_row)
    for e in range(entries):
        masks[e] = where(code_row == e + 1, 1.0, 0.0).astype(BF16)
    masks[entries] = where(seg_row == open_id, 1.0, 0.0).astype(BF16)
    first_row = where(seg_row == before, 1.0, 0.0)
    masks[entries + 1] = first_row.astype(BF16)
    any_first = jnp.max(first_row[:1])
    first[...] = where(seg_col == before, 1.0, 0.0)
    row = lax.broadcasted_iota(I32, (length, length), 0)
    col = lax.broadcasted_iota(I32, (length, length), 1)
    same = jnp.concatenate([seg_col] * (length // width), axis=1) == seg_row[:1]
    sums[:length] = where(row >= col, 1.0, 0.0).astype(BF16)
    sums[length:] = where(same & (col > row), 1.0, 0.0).astype(BF16)
    strict[...] = where(same & (row > col), 1.0, 0.0)
    lower[...] = where(same & (row >= col), 1.0, 0.0)
    hrow, hcol = row[:half, :half], col[:half, :half]
    depth = jnp.zeros((half, half), F32)
    size = BASE
    while size < half:
        depth = depth + where(hrow // size != hcol // size, 1.0, 0.0)
        size *= 2
    level[...] = depth

    small[0].wait()
    betas[...] = jax.nn.sigmoid(beta_raw[...].astype(F32))
    small[1].wait()

    @pl.when(me == 0)
    def _():
        for h in range(heads):
            state_in[h] = jnp.zeros((width, width), BF16)

    def prepare(p):
        for i in range(PAIR):
            h = p * PAIR + i
            cols = pl.ds(pl.multiple_of(h * width, width), width)
            q = unit(qv[:, cols].astype(F32))
            k = unit(kv[:, cols].astype(F32))
            yield None
            x = fv[:, cols].astype(F32)
            soft = jnp.maximum(x, 0.0) + jnp.log(1.0 + jnp.exp(-jnp.abs(x)))
            decay = -(rate[:, cols] * soft)
            summed = dot(sums[...], wide(decay))
            summed = summed[:, :width] + summed[:, width:]
            cum = summed[:length]
            yield None
            decayed = jnp.exp(cum) * first[...]
            beta = betas[pl.ds(h, 1), :]
            query_s[h] = q * decayed
            right_s[h] = jnp.concatenate([vv[:, cols], (k * decayed).astype(BF16)], axis=1)
            keep_s[h, :1] = jnp.exp(jnp.sum(first[...] * decay, axis=0, keepdims=True)) * any_first
            ended_s[h] = ((k * jnp.exp(summed[length:])).T * beta).astype(BF16)
            yield None
            cum0, cum1 = cum[:half], cum[half:]
            k0, k1, q0, q1 = k[:half], k[half:], q[:half], q[half:]
            mid0 = 0.5 * (cum0[:1] + cum0[-1:])
            mid1 = 0.5 * (cum1[:1] + cum1[-1:])
            up0, up1 = jnp.exp(cum0 - mid0), jnp.exp(cum1 - mid1)
            low0 = (k0 * jnp.exp(mid0 - cum0)).astype(BF16)
            low1 = jnp.concatenate([k0 * jnp.exp(mid1 - cum0), k1 * jnp.exp(mid1 - cum1)], axis=0).astype(BF16)
            block0 = dot(wide(jnp.concatenate([k0 * up0, q0 * up0], axis=0)), twice(low0, 1), NT)
            block1 = dot(wide(jnp.concatenate([k1 * up1, q1 * up1], axis=0)), twice(low1, 1), NT)
            yield None
            beta0, beta1 = beta[:, :half], beta[:, half:]
            mat_s[h, 0] = where(strict[:half, :half] > 0.0, block0[:half], 0.0) * beta0
            mat_s[h, 1] = where(strict[half:, half:] > 0.0, block1[:half, half:], 0.0) * beta1
            link_s[h] = wide(where(strict[half:, :half] > 0.0, block1[:half, :half], 0.0) * beta0)
            reading0 = where(lower[:half, :half] > 0.0, block0[half:], 0.0) * beta0
            reading1 = where(lower[half:, :] > 0.0, block1[half:], 0.0) * beta
            reading_s[h] = jnp.concatenate(
                [jnp.concatenate([reading0, jnp.zeros_like(reading0)], axis=1), reading1], axis=0).astype(BF16)
            yield None

    def local_pair(p, ahead):
        following = prepare(ahead)
        mats = [mat_s[p * PAIR + i, b] for i in range(PAIR) for b in range(2)]
        inverses = None
        for inverses in block_inverses(mats, level[...]):
            next(following, None)
        for _ in following:
            pass
        hr = lax.broadcasted_iota(I32, (width, width), 0)
        hc = lax.broadcasted_iota(I32, (width, width), 1)
        heads_of = [p * PAIR + i for i in range(PAIR)]
        right = [right_s[h] for h in heads_of]
        u0 = [dot(wide(inverses[2 * i]), twice(right[i][:half], 0)).astype(BF16) for i in range(PAIR)]
        rest = [right[i][half:].astype(F32) - dot(link_s[h], twice(u0[i], 0)) for i, h in enumerate(heads_of)]
        u1 = [dot(wide(inverses[2 * i + 1]), twice(rest[i].astype(BF16), 0)).astype(BF16) for i in range(PAIR)]
        for i, h in enumerate(heads_of):
            u = jnp.concatenate([u0[i], u1[i]], axis=0)
            chunks = ended_s[h].reshape(width // 16, 16, length)
            pick = lambda e: (chunks * masks[e][None]).reshape(width, length)
            states = dot(jnp.concatenate([pick(e) for e in range(entries + 1)], axis=0), u[:, :width])
            for c in range(owned):
                own[h, c] = states[c * width:(c + 1) * width].astype(BF16)
            for c in range(lanes):
                e = owned + c
                up_out[h, c] = states[e * width:(e + 1) * width].astype(BF16)
                e = owned + lanes + c
                dn_out[h, c] = states[e * width:(e + 1) * width].astype(BF16)
            tail[h] = states[entries * width:]
            through = dot(pick(entries + 1), u[:, width:])
            mapcorr[h, :width] = (where(hr == hc, keep_s[h, :1], 0.0) - through).astype(BF16)
            read = dot(reading_s[h], u)
            local[h] = read[:, :width]
            mapcorr[h, width:] = (query_s[h] - read[:, width:]).astype(BF16)

    def relay(p):
        for i in range(PAIR):
            h = p * PAIR + i

            @pl.when(has_down)
            def _():
                state_copy(h).wait_recv()

            applied = dot(mapcorr[h, :width], state_in[h])
            state_out[h] = (tail[h] + open_flag * applied).astype(BF16)

            @pl.when(has_up)
            def _():
                state_copy(h).start()

            moved[h] = applied.astype(BF16)

    def finish_heads(p):
        for i in range(PAIR):
            h = p * PAIR + i
            out = local[h] + dot(mapcorr[h, width:], state_in[h])
            cols = pl.ds(pl.multiple_of(h * width, width), width)
            scale = lax.rsqrt(jnp.mean(out * out, axis=-1, keepdims=True) + 1e-05)
            hidden[:, cols] = (out * scale * gain[...] * jax.nn.sigmoid(gate[:, cols].astype(F32))).astype(BF16)

    def shifted(own_part, entry, h, terms):
        value = own_part.astype(F32) + table[entry] * moved[h].astype(F32)
        for index, part in terms:
            value = value + table[index] * part.astype(F32)
        return value.astype(BF16)

    def up_flow(h):
        for c in range(lanes):
            up_copy(h, c).wait_recv()

            @pl.when(me < n - 2)
            def _():
                up_out[h, c] = shifted(up_out[h, c], owned + c, h, [(up_base + c * span, up_in[h, c])])
                up_copy(h, c).start()

        @pl.when(me == n - 2)
        def _():
            for k in range(owned):
                up_out[h, k] = shifted(up_out[h, k], owned + k, h,
                                       [(up_base + c * span + 1 + owned + k, up_in[h, c]) for c in range(lanes)])
                up_copy(h, k).start()

    def dn_lane_flow(h, c):
        @pl.when(me < n - 1)
        def _():
            dn_copy(h, c).wait_recv()
            dn_out[h, c] = shifted(dn_out[h, c], owned + lanes + c, h, [(dn_base + c * span, dn_in[h, c])])

        if c == lanes - 1:
            @pl.when(me == n - 1)
            def _():
                dn_out[h, c] = shifted(dn_out[h, c], owned + lanes + c, h, [])

        dn_copy(h, c).start()

    def dn_last_flow(h):
        for c in range(lanes):
            dn_copy(h, c).wait_recv()
        for k in range(owned):
            dn_out[h, k] = shifted(dn_out[h, k], owned + lanes + k, h,
                                   [(dn_base + c * span + 1 + owned + k, dn_in[h, c]) for c in range(lanes)])
            dn_copy(h, k).start()

    def settle(h):
        for k in range(owned):
            ups = [(up_base + c * span + 1 + k, up_in, c) for c in range(lanes)]
            downs = [(dn_base + c * span + 1 + k, dn_in, c) for c in range(lanes)]

            @pl.when(inner)
            def _():
                slot_ref[k, h] = shifted(own[h, k], k, h, [(x, ref[h, c]) for x, ref, c in ups + downs])

            @pl.when(me == 0)
            def _():
                dn_copy(h, k).wait_recv()
                slot_ref[k, h] = (own[h, k].astype(F32) + dn_in[h, k].astype(F32)).astype(BF16)

            @pl.when(me == n - 1)
            def _():
                up_copy(h, k).wait_recv()
                slot_ref[k, h] = (own[h, k].astype(F32) + table[k] * moved[h].astype(F32)
                                  + up_in[h, k].astype(F32)).astype(BF16)

    def project():
        if (2 * piece) % 128 == 0:
            for j in range(nh - 1, -1, -1):
                to = lax.rem(head_at + j, nh)
                cols = pl.ds(pl.multiple_of(to * 2 * piece, 128), 2 * piece)
                full = dot(hidden[...], weight[:, cols])
                parts[2 * to] = full[:, :piece].astype(BF16)
                parts[2 * to + 1] = full[:, piece:].astype(BF16)
                pair_copy(to).start()
        else:
            full = dot(hidden[...], weight[...])
            for d in range(2 * nh):
                parts[d] = full[:, d * piece:(d + 1) * piece].astype(BF16)
            for j in range(nh):
                pair_copy(j).start()

    def combine():
        for j in range(nh - 1, 0, -1):
            to = lax.rem(head_at + j, nh)
            pair_copy(to).wait_recv()
            sums_out[j] = (parts[2 * to + rep_at].astype(F32) + pair_in[to].astype(F32)).astype(BF16)
            cross_copy(j).start()
        pair_copy(head_at).wait_recv()

    def conclude():
        result = parts[2 * head_at + rep_at].astype(F32) + pair_in[head_at].astype(F32)
        for j in range(1, nh):
            cross_copy(j).wait_recv()
            result = result + cross_in[j].astype(F32)
        layer_ref[...] = result.T.astype(BF16)

    below = n - 1 - me
    dn_last = 3 * n - 4
    settle_base = jnp.maximum(pairs + 1 + me, n - 2 + 2 * below)
    settle_base = where(me == 1, jnp.maximum(settle_base, dn_last), settle_base)
    settle_base = where(me == 0, dn_last + 1, settle_base)
    ticks = pairs + max(pairs + n, 3 * n - 4, dn_last + 1)

    def valid(x, limit):
        return (x >= 0) & (x < limit)

    def advance(t, carry):
        ahead = jnp.minimum(t + 1, pairs - 1)

        @pl.when(t + 1 < pairs)
        def _():
            for i in range(4):
                pair_load(ahead, i).wait()

        @pl.when(t < pairs)
        def _():
            local_pair(t, ahead)

        @pl.when((t == 0) & inner)
        def _():
            pl.semaphore_wait(barrier, nh + 2)

        @pl.when((t == 0) & jnp.logical_not(inner))
        def _():
            pl.semaphore_wait(barrier, nh + 1)

        p = t - me
        hu = t - me - 1

        @pl.when(inner & valid(hu, heads))
        def _():
            up_flow(hu)

        @pl.when(p == pairs)
        def _():
            combine()

        @pl.when(valid(p, pairs))
        def _():
            relay(p)

        @pl.when((me == 0) & (t < pairs))
        def _():
            for c in range(lanes):
                up_copy(t, c).start()

        @pl.when((me == 0) & (t == pairs - 1))
        def _():
            for h in range(pairs, heads):
                for c in range(lanes):
                    up_copy(h, c).start()

        @pl.when((me == n - 1) & (t < pairs))
        def _():
            for i in range(PAIR):
                for c in range(lanes - 1):
                    dn_copy(t * PAIR + i, c).start()

        @pl.when((me == n - 1) & valid(p, pairs))
        def _():
            for i in range(PAIR):
                dn_lane_flow(p * PAIR + i, lanes - 1)

        early = t - (n - 4) - 2 * below

        @pl.when(inner & (me > 1) & valid(early, pairs))
        def _():
            for i in range(PAIR):
                for c in range(lanes - 1):
                    dn_lane_flow(early * PAIR + i, c)

        @pl.when(valid(p, pairs))
        def _():
            finish_heads(p)

        @pl.when(p == pairs - 1)
        def _():
            small[4].wait()
            project()

        late = t - n + 2 - 2 * below

        @pl.when(inner & (me > 1) & valid(late, pairs))
        def _():
            for i in range(PAIR):
                dn_lane_flow(late * PAIR + i, lanes - 1)

        last = t - dn_last

        @pl.when((me == 1) & valid(last, pairs))
        def _():
            for i in range(PAIR):
                dn_last_flow(last * PAIR + i)

        @pl.when(t == ticks - 1)
        def _():
            conclude()

        ps = t - settle_base

        @pl.when(valid(ps, pairs))
        def _():
            for i in range(PAIR):
                settle(ps * PAIR + i)

        return carry

    small[2].wait()
    small[3].wait()
    for i in range(4):
        pair_load(0, i).wait()
    for _ in prepare(0):
        pass
    lax.fori_loop(0, ticks, advance, 0)

    for j in range(nh):
        pair_copy(j).wait_send()
    for j in range(1, nh):
        cross_copy(j).wait_send()

    few = pl.ds(0, owned)

    @pl.when(has_up)
    def _():
        remote(state_out, state_in, st_send, st_recv.at[0], up).wait_send()

    @pl.when(me < n - 2)
    def _():
        remote(up_out, up_in, up_send, up_recv.at[0, 0], up).wait_send()

    @pl.when(me == n - 2)
    def _():
        remote(up_out.at[:, few], up_in.at[:, few], up_send, up_recv.at[0, 0], up).wait_send()

    @pl.when(me > 1)
    def _():
        remote(dn_out, dn_in, dn_send, dn_recv.at[0, 0], down).wait_send()

    @pl.when(me == 1)
    def _():
        remote(dn_out.at[:, few], dn_in.at[:, few], dn_send, dn_recv.at[0, 0], down).wait_send()


def emit_kernel(layer_ref, slot_ref, layer_out, slot_out, layer, slots, sems):
    count = slots.shape[0]
    loads = [pltpu.make_async_copy(layer_ref, layer, sems.at[0])]
    stores = [pltpu.make_async_copy(layer, layer_out, sems.at[1])]
    for c in range(count):
        loads.append(pltpu.make_async_copy(slot_ref.at[c], slots.at[c], sems.at[2 + c]))
        stores.append(pltpu.make_async_copy(slots.at[c], slot_out.at[c], sems.at[2 + count + c]))
    for load in loads:
        load.start()
    for load, store in zip(loads, stores):
        load.wait()
        store.start()
    for store in stores:
        store.wait()


def emit(layer, slots):
    hbm = pl.BlockSpec(memory_space=pl.ANY)
    return pl.pallas_call(
        emit_kernel,
        out_shape=(jax.ShapeDtypeStruct(layer.shape, layer.dtype), jax.ShapeDtypeStruct(slots.shape, slots.dtype)),
        in_specs=[hbm, hbm],
        out_specs=(hbm, hbm),
        scratch_shapes=[pltpu.VMEM(layer.shape, layer.dtype), pltpu.VMEM(slots.shape, slots.dtype),
                        pltpu.SemaphoreType.DMA((2 + 2 * slots.shape[0],))],
        compiler_params=pltpu.CompilerParams(vmem_limit_bytes=60 << 20),
        name="emit",
    )(layer, slots)


def fused(starts, slots, q, k, v, f, rate, beta, gates, gain, weight):
    n = lax.axis_size("seq")
    nh = lax.axis_size("head")
    length, total = q.shape
    heads = beta.shape[1]
    width = total // heads
    half = length // 2
    depth, model = weight.shape
    piece = model // (2 * nh)
    owned = slots.shape[0] // n
    lanes = max(min(ENDS_MAX * (p + 1), owned * (n - 1 - p)) for p in range(n - 1))
    entries = owned + 2 * lanes
    vmem = pl.BlockSpec(memory_space=pltpu.VMEM)
    smem = pl.BlockSpec(memory_space=pltpu.SMEM)
    hbm = pl.BlockSpec(memory_space=pl.ANY)
    dma = pltpu.SemaphoreType.DMA
    cube = pltpu.VMEM((heads, width, width), BF16)
    flow = pltpu.VMEM((heads, lanes, width, width), BF16)
    slab = pltpu.VMEM((length, total), BF16)
    return pl.pallas_call(
        functools.partial(fused_kernel, n, nh, lanes),
        out_shape=(jax.ShapeDtypeStruct((piece, length), BF16),
                   jax.ShapeDtypeStruct((owned, heads, width, width), BF16)),
        in_specs=[smem, smem] + [hbm] * 9,
        out_specs=(vmem, vmem),
        scratch_shapes=[
            slab, slab, slab, slab, slab,
            pltpu.VMEM((1, total), F32),
            pltpu.VMEM((heads, length), BF16),
            pltpu.VMEM((1, width), F32),
            pltpu.VMEM((depth, model), BF16),
            pltpu.VMEM((2 * length, length), BF16),
            pltpu.VMEM((length, length), F32),
            pltpu.VMEM((length, length), F32),
            pltpu.VMEM((half, half), F32),
            pltpu.VMEM((length, width), F32),
            pltpu.VMEM((entries + 2, 16, length), BF16),
            pltpu.VMEM((heads, length), F32),
            pltpu.SMEM((entries + 2 * lanes * (1 + 2 * owned),), F32),
            pltpu.VMEM((heads, 2, half, half), F32),
            pltpu.VMEM((heads, half, 2 * half), BF16),
            pltpu.VMEM((heads, length, length), BF16),
            pltpu.VMEM((heads, length, 2 * width), BF16),
            pltpu.VMEM((heads, length, width), F32),
            pltpu.VMEM((heads, width, length), BF16),
            pltpu.VMEM((heads, 8, width), F32),
            pltpu.VMEM((heads, length, width), F32),
            pltpu.VMEM((heads, width + length, width), BF16),
            pltpu.VMEM((heads, width, width), F32),
            pltpu.VMEM((heads, owned, width, width), BF16),
            cube,
            slab,
            cube, cube,
            flow, flow, flow, flow,
            pltpu.VMEM((2 * nh, length, piece), BF16),
            pltpu.VMEM((nh, length, piece), BF16),
            pltpu.VMEM((nh, length, piece), BF16),
            pltpu.VMEM((nh, length, piece), BF16),
            dma((heads // PAIR, 4)), dma((5,)),
            dma, dma((heads,)), dma, dma((heads, lanes)), dma, dma((heads, lanes)),
            dma((nh,)), dma((nh,)), dma((nh,)), dma((nh,)),
        ],
        compiler_params=pltpu.CompilerParams(collective_id=0, has_side_effects=True,
                                             vmem_limit_bytes=60 << 20),
        name="fused",
    )(starts, slots, q, k, v, f, rate.reshape(1, -1), beta.T, gates, gain.reshape(1, -1), weight)


def per_device(query_proj, key_proj, value_proj, forget_logits, decay_rate, beta_logits,
               gate_logits, norm_gain, out_weight, stream_starts, stream_slots):
    layer, slots = fused(stream_starts, stream_slots, query_proj, key_proj, value_proj, forget_logits, decay_rate,
                 beta_logits, gate_logits, norm_gain, out_weight)
    layer, slots = emit(layer, slots)
    return layer.T, slots


def solution(mesh):
    rows = P(("groups", "seq"), ("head", "rep"))
    in_specs = (rows, rows, rows, rows, P(("head", "rep")), rows, rows, P(),
                P(("head", "rep"), None), P("groups"), P("groups"))
    out_specs = (rows, P(("groups", "seq"), ("head", "rep"), None, None))
    return jax.shard_map(per_device, mesh=mesh, in_specs=in_specs, out_specs=out_specs, check_vma=False)
```

```python
import functools
import jax
import jax.numpy as jnp
from jax import lax
from jax.experimental import pallas as pl
from jax.experimental.pallas import tpu as pltpu
from jax.sharding import PartitionSpec as P

ENDS_MAX = 4
PAIR = 2
BASE = 16
F32 = jnp.float32
BF16 = jnp.bfloat16
I32 = jnp.int32
NN = (((1,), (0,)), ((), ()))
NT = (((1,), (1,)), ((), ()))


def halves(x):
    high = x.astype(BF16)
    return high, (x - high.astype(F32)).astype(BF16)


def dot(a, b, dims=NN):
    return lax.dot_general(a, b, dims, preferred_element_type=F32)


def wide(x):
    return jnp.concatenate(halves(x), axis=1)


def twice(x, axis):
    return jnp.concatenate([x, x], axis=axis)


def mm4(a, b):
    both = dot(a, twice(b, 0))
    half = both.shape[1] // 2
    return both[:, :half] + both[:, half:]


def unit(x):
    return x * lax.rsqrt(jnp.sum(x * x, axis=-1, keepdims=True) + 1e-06)


def block_inverses(mats, level):
    size = mats[0].shape[0]
    row = lax.broadcasted_iota(I32, (size, size), 0)
    col = lax.broadcasted_iota(I32, (size, size), 1)
    eye = (row == col).astype(F32)
    powers = [jnp.where(level == 0.0, m, 0.0) for m in mats]
    result = [eye - p for p in powers]
    splits = [wide(p) for p in powers]
    powers = [mm4(s, s) for s in splits]
    yield None
    width = 4
    while width < BASE:
        splits = [wide(p) for p in powers]
        both = [mm4(jnp.concatenate([wide(r), s], axis=0), s) for r, s in zip(result, splits)]
        result = [r + b[:size] for r, b in zip(result, both)]
        powers = [b[size:] for b in both]
        width *= 2
        yield None
    splits = [wide(p) for p in powers]
    result = [r + mm4(wide(r), s) for r, s in zip(result, splits)]
    yield None
    width = BASE
    step = 1
    while width < size:
        splits = [r.astype(BF16) for r in result]
        mids = [dot(jnp.where(level == float(step), m, 0.0).astype(BF16), s) for m, s in zip(mats, splits)]
        yield None
        result = [r - dot(s, t.astype(BF16)) for r, s, t in zip(result, splits, mids)]
        width *= 2
        step += 1
        yield None
    yield result


def fused_kernel(n, nh, lanes, *refs):
    (starts_hbm, slots_hbm, q_hbm, k_hbm, v_hbm, f_hbm, rate_hbm, beta_hbm, gate_hbm, gain_hbm, weight_hbm,
     layer_hbm, slot_hbm,
     layer_ref, slot_ref, out_sem,
     qv, kv, vv, fv, gate, rate, beta_raw, gain, weight,
     sums, strict, lower, level, first, masks, betas, table,
     mat_s, link_s, reading_s, right_s, query_s, ended_s, keep_s,
     local, mapcorr, tail, own, moved, hidden, state_in, state_out,
     up_in, up_out, dn_in, dn_out, parts, pair_in, sums_out, cross_in,
     starts_ref, slots_ref, load_sem, misc_sem,
     st_send, st_recv, up_send, up_recv, dn_send, dn_recv, p_send, p_recv, c_send, c_recv) = refs
    length, total = qv.shape
    heads = own.shape[0]
    owned = own.shape[1]
    width = total // heads
    half = length // 2
    pairs = heads // PAIR
    streams = starts_ref.shape[0]
    piece = layer_ref.shape[0]
    me = lax.axis_index("seq")
    head_at = lax.axis_index("head")
    rep_at = lax.axis_index("rep")
    mesh_id = pl.DeviceIdType.MESH
    up, down, partner = {"seq": me + 1}, {"seq": me - 1}, {"rep": 1 - rep_at}
    has_up, has_down = me < n - 1, me > 0
    inner = has_up & has_down

    def pair_load(p, i):
        src, dst = ((f_hbm, fv), (k_hbm, kv), (q_hbm, qv), (v_hbm, vv))[i]
        cols = pl.ds(pl.multiple_of(p * PAIR * width, width), PAIR * width)
        return pltpu.make_async_copy(src.at[:, cols], dst.at[:, cols], load_sem.at[p, i])

    small = [pltpu.make_async_copy(src, dst, misc_sem.at[i]) for i, (src, dst) in enumerate(
        ((beta_hbm, beta_raw), (rate_hbm, rate), (gain_hbm, gain), (gate_hbm, gate), (weight_hbm, weight),
         (starts_hbm, starts_ref), (slots_hbm, slots_ref)))]
    for copy in small[5:] + small[:3]:
        copy.start()
    for p in range(pairs):
        for i in range(4):
            pair_load(p, i).start()
    for copy in small[3:5]:
        copy.start()

    barrier = pltpu.get_barrier_semaphore()

    @pl.when(has_up)
    def _():
        pl.semaphore_signal(barrier, inc=1, device_id=up, device_id_type=mesh_id)

    @pl.when(has_down)
    def _():
        pl.semaphore_signal(barrier, inc=1, device_id=down, device_id_type=mesh_id)

    pl.semaphore_signal(barrier, inc=1, device_id=partner, device_id_type=mesh_id)
    for j in range(1, nh):
        pl.semaphore_signal(barrier, inc=1, device_id={"head": lax.rem(head_at + j, nh)}, device_id_type=mesh_id)

    def remote(src, dst, send, recv, target):
        return pltpu.make_async_remote_copy(src_ref=src, dst_ref=dst, send_sem=send, recv_sem=recv,
                                            device_id=target, device_id_type=mesh_id)

    def state_copy(h):
        return remote(state_out.at[h], state_in.at[h], st_send, st_recv.at[h], up)

    def up_copy(h, c):
        return remote(up_out.at[h, c], up_in.at[h, c], up_send, up_recv.at[h, c], up)

    def dn_copy(h, c):
        return remote(dn_out.at[h, c], dn_in.at[h, c], dn_send, dn_recv.at[h, c], down)

    def pair_copy(j):
        return remote(parts.at[2 * j + 1 - rep_at], pair_in.at[j], p_send.at[j], p_recv.at[j], partner)

    def cross_copy(j):
        return remote(sums_out.at[j], cross_in.at[j], c_send.at[j], c_recv.at[j],
                      {"head": lax.rem(head_at + j, nh)})

    for copy in small[5:]:
        copy.wait()
    anchor = me * length
    begins = [starts_ref[j] for j in range(streams)]
    slots = [slots_ref[j] for j in range(streams)]
    ends = begins[1:] + [n * length]
    count = lambda flags: sum(f.astype(I32) for f in flags)
    where = jnp.where
    end_at = [count([e > p * length for p in range(1, n)]) if isinstance(e, jax.Array) else jnp.int32(n - 1)
              for e in ends]
    dest = [count([s >= p * owned for p in range(1, n)]) for s in slots]
    here = [e == me for e in end_at]
    before = where(me == 0, -1, count([b <= anchor - 1 for b in begins]))
    open_id = 1 + count([e <= me for e in end_at])
    open_flag = 1.0 - where(count(here) > 0, 1.0, 0.0)

    def colours(order, crossing, free, idle, late):
        busy = [jnp.int32(idle)] * lanes
        result = [None] * streams
        for j in order:
            left = crossing(j)
            last = left & late(j)
            left = left & jnp.logical_not(last)
            pick_at = where(last, lanes - 1, -1)
            for c in range(lanes):
                pick = left & free(busy[c], end_at[j])
                pick_at = where(pick, c, pick_at)
                left = left & jnp.logical_not(pick)
                if c == lanes - 1:
                    pick = pick | last
                busy[c] = where(pick, dest[j], busy[c])
            result[j] = pick_at
        return result

    up_lane = colours(list(range(streams)), lambda j: dest[j] > end_at[j], lambda b, e: b <= e, 0,
                      lambda j: jnp.bool_(False))
    dn_lane = colours(list(range(streams))[::-1], lambda j: dest[j] < end_at[j], lambda b, e: b >= e, n,
                      lambda j: (end_at[j] == n - 1) & (begins[j] < (n - 1) * length))
    code = []
    for j in range(streams):
        home = where(dest[j] == me, slots[j] - me * owned + 1, 0)
        rise = where(me == n - 2, slots[j] - (n - 1) * owned, up_lane[j]) + 1 + owned
        rise = where(dest[j] > me, rise, 0)
        fall = where(me == 1, slots[j], dn_lane[j]) + 1 + owned + lanes
        fall = where(dest[j] < me, fall, 0)
        code.append(where(here[j], home + rise + fall, 0))
    begun = sum(where(before == j + 1, code[j], 0) for j in range(streams))
    entries = owned + 2 * lanes
    for e in range(entries):
        table[e] = where(begun == e + 1, 1.0, 0.0)
    at = entries
    span = 1 + 2 * owned
    for lane_of, came, goes, far in ((up_lane, lambda j: end_at[j] < me, lambda j: dest[j] > me, n - 1),
                                     (dn_lane, lambda j: end_at[j] > me, lambda j: dest[j] < me, 0)):
        lane_in = [where(came(j), lane_of[j], -1) for j in range(streams)]
        passing = [where(goes(j), lane_in[j], -1) for j in range(streams)]
        places = [passing] + [[where(slots[j] == at_slot, lane_in[j], -1) for j in range(streams)]
                              for at_slot in [me * owned + k for k in range(owned)] + [far * owned + k for k in range(owned)]]
        for c in range(lanes):
            for x, lane_list in enumerate(places):
                table[at + x] = where(count([y == c for y in lane_list]) > 0, 1.0, 0.0)
            at += span
    up_base, dn_base = entries, entries + lanes * span

    pos_row = lax.broadcasted_iota(I32, (16, length), 1) + anchor
    pos_col = lax.broadcasted_iota(I32, (length, width), 0) + anchor
    seg_row = jnp.zeros((16, length), I32)
    seg_col = jnp.zeros((length, width), I32)
    for j in range(streams):
        seg_row = seg_row + where(pos_row >= begins[j], 1, 0)
        seg_col = seg_col + where(pos_col >= begins[j], 1, 0)
    code_row = jnp.zeros((16, length), I32)
    for j in range(streams):
        code_row = where(seg_row == j + 1, code[j], code_row)
    for e in range(entries):
        masks[e] = where(code_row == e + 1, 1.0, 0.0).astype(BF16)
    masks[entries] = where(seg_row == open_id, 1.0, 0.0).astype(BF16)
    first_row = where(seg_row == before, 1.0, 0.0)
    masks[entries + 1] = first_row.astype(BF16)
    any_first = jnp.max(first_row[:1])
    first[...] = where(seg_col == before, 1.0, 0.0)
    row = lax.broadcasted_iota(I32, (length, length), 0)
    col = lax.broadcasted_iota(I32, (length, length), 1)
    same = jnp.concatenate([seg_col] * (length // width), axis=1) == seg_row[:1]
    sums[:length] = where(row >= col, 1.0, 0.0).astype(BF16)
    sums[length:] = where(same & (col > row), 1.0, 0.0).astype(BF16)
    strict[...] = where(same & (row > col), 1.0, 0.0)
    lower[...] = where(same & (row >= col), 1.0, 0.0)
    hrow, hcol = row[:half, :half], col[:half, :half]
    depth = jnp.zeros((half, half), F32)
    size = BASE
    while size < half:
        depth = depth + where(hrow // size != hcol // size, 1.0, 0.0)
        size *= 2
    level[...] = depth

    small[0].wait()
    betas[...] = jax.nn.sigmoid(beta_raw[...].astype(F32))
    small[1].wait()

    @pl.when(me == 0)
    def _():
        for h in range(heads):
            state_in[h] = jnp.zeros((width, width), BF16)

    def prepare(p):
        for i in range(PAIR):
            h = p * PAIR + i
            cols = pl.ds(pl.multiple_of(h * width, width), width)
            q = unit(qv[:, cols].astype(F32))
            k = unit(kv[:, cols].astype(F32))
            yield None
            x = fv[:, cols].astype(F32)
            soft = jnp.maximum(x, 0.0) + jnp.log(1.0 + jnp.exp(-jnp.abs(x)))
            decay = -(rate[:, cols] * soft)
            summed = dot(sums[...], wide(decay))
            summed = summed[:, :width] + summed[:, width:]
            cum = summed[:length]
            yield None
            decayed = jnp.exp(cum) * first[...]
            beta = betas[pl.ds(h, 1), :]
            query_s[h] = q * decayed
            right_s[h] = jnp.concatenate([vv[:, cols], (k * decayed).astype(BF16)], axis=1)
            keep_s[h, :1] = jnp.exp(jnp.sum(first[...] * decay, axis=0, keepdims=True)) * any_first
            ended_s[h] = ((k * jnp.exp(summed[length:])).T * beta).astype(BF16)
            yield None
            cum0, cum1 = cum[:half], cum[half:]
            k0, k1, q0, q1 = k[:half], k[half:], q[:half], q[half:]
            mid0 = 0.5 * (cum0[:1] + cum0[-1:])
            mid1 = 0.5 * (cum1[:1] + cum1[-1:])
            up0, up1 = jnp.exp(cum0 - mid0), jnp.exp(cum1 - mid1)
            low0 = (k0 * jnp.exp(mid0 - cum0)).astype(BF16)
            low1 = jnp.concatenate([k0 * jnp.exp(mid1 - cum0), k1 * jnp.exp(mid1 - cum1)], axis=0).astype(BF16)
            block0 = dot(wide(jnp.concatenate([k0 * up0, q0 * up0], axis=0)), twice(low0, 1), NT)
            block1 = dot(wide(jnp.concatenate([k1 * up1, q1 * up1], axis=0)), twice(low1, 1), NT)
            yield None
            beta0, beta1 = beta[:, :half], beta[:, half:]
            mat_s[h, 0] = where(strict[:half, :half] > 0.0, block0[:half], 0.0) * beta0
            mat_s[h, 1] = where(strict[half:, half:] > 0.0, block1[:half, half:], 0.0) * beta1
            link_s[h] = wide(where(strict[half:, :half] > 0.0, block1[:half, :half], 0.0) * beta0)
            reading0 = where(lower[:half, :half] > 0.0, block0[half:], 0.0) * beta0
            reading1 = where(lower[half:, :] > 0.0, block1[half:], 0.0) * beta
            reading_s[h] = jnp.concatenate(
                [jnp.concatenate([reading0, jnp.zeros_like(reading0)], axis=1), reading1], axis=0).astype(BF16)
            yield None

    def local_pair(p, ahead):
        following = prepare(ahead)
        mats = [mat_s[p * PAIR + i, b] for i in range(PAIR) for b in range(2)]
        inverses = None
        for inverses in block_inverses(mats, level[...]):
            next(following, None)
        for _ in following:
            pass
        hr = lax.broadcasted_iota(I32, (width, width), 0)
        hc = lax.broadcasted_iota(I32, (width, width), 1)
        heads_of = [p * PAIR + i for i in range(PAIR)]
        right = [right_s[h] for h in heads_of]
        u0 = [dot(wide(inverses[2 * i]), twice(right[i][:half], 0)).astype(BF16) for i in range(PAIR)]
        rest = [right[i][half:].astype(F32) - dot(link_s[h], twice(u0[i], 0)) for i, h in enumerate(heads_of)]
        u1 = [dot(wide(inverses[2 * i + 1]), twice(rest[i].astype(BF16), 0)).astype(BF16) for i in range(PAIR)]
        for i, h in enumerate(heads_of):
            u = jnp.concatenate([u0[i], u1[i]], axis=0)
            chunks = ended_s[h].reshape(width // 16, 16, length)
            pick = lambda e: (chunks * masks[e][None]).reshape(width, length)
            states = dot(jnp.concatenate([pick(e) for e in range(entries + 1)], axis=0), u[:, :width])
            for c in range(owned):
                own[h, c] = states[c * width:(c + 1) * width].astype(BF16)
            for c in range(lanes):
                e = owned + c
                up_out[h, c] = states[e * width:(e + 1) * width].astype(BF16)
                e = owned + lanes + c
                dn_out[h, c] = states[e * width:(e + 1) * width].astype(BF16)
            tail[h] = states[entries * width:]
            through = dot(pick(entries + 1), u[:, width:])
            mapcorr[h, :width] = (where(hr == hc, keep_s[h, :1], 0.0) - through).astype(BF16)
            read = dot(reading_s[h], u)
            local[h] = read[:, :width]
            mapcorr[h, width:] = (query_s[h] - read[:, width:]).astype(BF16)

    def relay(p):
        for i in range(PAIR):
            h = p * PAIR + i

            @pl.when(has_down)
            def _():
                state_copy(h).wait_recv()

            applied = dot(mapcorr[h, :width], state_in[h])
            state_out[h] = (tail[h] + open_flag * applied).astype(BF16)

            @pl.when(has_up)
            def _():
                state_copy(h).start()

            moved[h] = applied.astype(BF16)

    def finish_heads(p):
        for i in range(PAIR):
            h = p * PAIR + i
            out = local[h] + dot(mapcorr[h, width:], state_in[h])
            cols = pl.ds(pl.multiple_of(h * width, width), width)
            scale = lax.rsqrt(jnp.mean(out * out, axis=-1, keepdims=True) + 1e-05)
            hidden[:, cols] = (out * scale * gain[...] * jax.nn.sigmoid(gate[:, cols].astype(F32))).astype(BF16)

    def shifted(own_part, entry, h, terms):
        value = own_part.astype(F32) + table[entry] * moved[h].astype(F32)
        for index, part in terms:
            value = value + table[index] * part.astype(F32)
        return value.astype(BF16)

    def up_flow(h):
        for c in range(lanes):
            up_copy(h, c).wait_recv()

            @pl.when(me < n - 2)
            def _():
                up_out[h, c] = shifted(up_out[h, c], owned + c, h, [(up_base + c * span, up_in[h, c])])
                up_copy(h, c).start()

        @pl.when(me == n - 2)
        def _():
            for k in range(owned):
                up_out[h, k] = shifted(up_out[h, k], owned + k, h,
                                       [(up_base + c * span + 1 + owned + k, up_in[h, c]) for c in range(lanes)])
                up_copy(h, k).start()

    def dn_lane_flow(h, c):
        @pl.when(me < n - 1)
        def _():
            dn_copy(h, c).wait_recv()
            dn_out[h, c] = shifted(dn_out[h, c], owned + lanes + c, h, [(dn_base + c * span, dn_in[h, c])])

        if c == lanes - 1:
            @pl.when(me == n - 1)
            def _():
                dn_out[h, c] = shifted(dn_out[h, c], owned + lanes + c, h, [])

        dn_copy(h, c).start()

    def dn_last_flow(h):
        for c in range(lanes):
            dn_copy(h, c).wait_recv()
        for k in range(owned):
            dn_out[h, k] = shifted(dn_out[h, k], owned + lanes + k, h,
                                   [(dn_base + c * span + 1 + owned + k, dn_in[h, c]) for c in range(lanes)])
            dn_copy(h, k).start()

    def store_layer():
        return pltpu.make_async_copy(layer_ref, layer_hbm, out_sem.at[pairs])

    def store_slots(p):
        some = pl.ds(p * PAIR, PAIR)
        return pltpu.make_async_copy(slot_ref.at[:, some], slot_hbm.at[:, some], out_sem.at[p])

    def settle(h):
        for k in range(owned):
            ups = [(up_base + c * span + 1 + k, up_in, c) for c in range(lanes)]
            downs = [(dn_base + c * span + 1 + k, dn_in, c) for c in range(lanes)]

            @pl.when(inner)
            def _():
                slot_ref[k, h] = shifted(own[h, k], k, h, [(x, ref[h, c]) for x, ref, c in ups + downs])

            @pl.when(me == 0)
            def _():
                dn_copy(h, k).wait_recv()
                slot_ref[k, h] = (own[h, k].astype(F32) + dn_in[h, k].astype(F32)).astype(BF16)

            @pl.when(me == n - 1)
            def _():
                up_copy(h, k).wait_recv()
                slot_ref[k, h] = (own[h, k].astype(F32) + table[k] * moved[h].astype(F32)
                                  + up_in[h, k].astype(F32)).astype(BF16)

    def project():
        if (2 * piece) % 128 == 0:
            for j in range(nh - 1, -1, -1):
                to = lax.rem(head_at + j, nh)
                cols = pl.ds(pl.multiple_of(to * 2 * piece, 128), 2 * piece)
                full = dot(hidden[...], weight[:, cols])
                parts[2 * to] = full[:, :piece].astype(BF16)
                parts[2 * to + 1] = full[:, piece:].astype(BF16)
                pair_copy(to).start()
        else:
            full = dot(hidden[...], weight[...])
            for d in range(2 * nh):
                parts[d] = full[:, d * piece:(d + 1) * piece].astype(BF16)
            for j in range(nh):
                pair_copy(j).start()

    def combine():
        for j in range(nh - 1, 0, -1):
            to = lax.rem(head_at + j, nh)
            pair_copy(to).wait_recv()
            sums_out[j] = (parts[2 * to + rep_at].astype(F32) + pair_in[to].astype(F32)).astype(BF16)
            cross_copy(j).start()
        pair_copy(head_at).wait_recv()

    def conclude():
        result = parts[2 * head_at + rep_at].astype(F32) + pair_in[head_at].astype(F32)
        for j in range(1, nh):
            cross_copy(j).wait_recv()
            result = result + cross_in[j].astype(F32)
        layer_ref[...] = result.T.astype(BF16)
        store_layer().start()

    below = n - 1 - me
    dn_last = 3 * n - 6
    settle_base = jnp.maximum(pairs + 1 + me, n - 1 + 2 * below)
    settle_base = where(me == 1, jnp.maximum(settle_base, dn_last + 1), settle_base)
    settle_base = where(me == n - 1, pairs + n, settle_base)
    settle_base = where(me == 0, dn_last + 2, settle_base)
    ticks = pairs + max(pairs + n, 3 * n - 5, dn_last + 2)

    def shifted_tick(x, extra):
        return where(x < pairs - 1, x, where(x < pairs - 1 + extra, -1, x - extra))

    def valid(x, limit):
        return (x >= 0) & (x < limit)

    def advance(t, carry):
        ahead = jnp.minimum(t + 1, pairs - 1)

        @pl.when(t + 1 < pairs)
        def _():
            for i in range(4):
                pair_load(ahead, i).wait()

        @pl.when(t < pairs)
        def _():
            local_pair(t, ahead)

        @pl.when((t == 0) & inner)
        def _():
            pl.semaphore_wait(barrier, nh + 2)

        @pl.when((t == 0) & jnp.logical_not(inner))
        def _():
            pl.semaphore_wait(barrier, nh + 1)

        p = t - me
        hu = t - me

        @pl.when(p == pairs)
        def _():
            combine()

        @pl.when(valid(p, pairs))
        def _():
            relay(p)

        @pl.when((me == 0) & (t < pairs))
        def _():
            for c in range(lanes):
                up_copy(t, c).start()

        @pl.when((me == 0) & (t == pairs - 1))
        def _():
            for h in range(pairs, heads):
                for c in range(lanes):
                    up_copy(h, c).start()

        @pl.when((me == n - 1) & (t < pairs))
        def _():
            for i in range(PAIR):
                for c in range(lanes - 1):
                    dn_copy(t * PAIR + i, c).start()

        @pl.when((me == n - 1) & valid(p, pairs))
        def _():
            for i in range(PAIR):
                dn_lane_flow(p * PAIR + i, lanes - 1)

        early = shifted_tick(t - (n - 4) - 2 * below, 0)

        @pl.when(inner & (me > 1) & valid(early, pairs))
        def _():
            for i in range(PAIR):
                for c in range(lanes - 1):
                    dn_lane_flow(early * PAIR + i, c)

        @pl.when(valid(p, pairs))
        def _():
            finish_heads(p)

        @pl.when(p == pairs - 1)
        def _():
            small[4].wait()
            project()

        @pl.when(inner & valid(hu, heads))
        def _():
            up_flow(hu)

        late = t - n + 2 - 2 * below - 0

        @pl.when(inner & (me > 1) & valid(late, pairs))
        def _():
            for i in range(PAIR):
                dn_lane_flow(late * PAIR + i, lanes - 1)

        last = shifted_tick(t - dn_last, 1)

        @pl.when((me == 1) & valid(last, pairs))
        def _():
            for i in range(PAIR):
                dn_last_flow(last * PAIR + i)

        @pl.when(t == where(me == 0, 9, where(me == n - 1, ticks - 2, ticks - 1)))
        def _():
            conclude()

        ps = t - settle_base

        @pl.when(valid(ps, pairs))
        def _():
            for i in range(PAIR):
                settle(ps * PAIR + i)
            store_slots(ps).start()

        return carry

    small[2].wait()
    small[3].wait()
    for i in range(4):
        pair_load(0, i).wait()
    for _ in prepare(0):
        pass
    lax.fori_loop(0, ticks, advance, 0)

    for j in range(nh):
        pair_copy(j).wait_send()
    for j in range(1, nh):
        cross_copy(j).wait_send()

    few = pl.ds(0, owned)
    store_layer().wait()
    for p in range(pairs):
        store_slots(p).wait()

    @pl.when(has_up)
    def _():
        remote(state_out, state_in, st_send, st_recv.at[0], up).wait_send()

    @pl.when(me < n - 2)
    def _():
        remote(up_out, up_in, up_send, up_recv.at[0, 0], up).wait_send()

    @pl.when(me == n - 2)
    def _():
        remote(up_out.at[:, few], up_in.at[:, few], up_send, up_recv.at[0, 0], up).wait_send()

    @pl.when(me > 1)
    def _():
        remote(dn_out, dn_in, dn_send, dn_recv.at[0, 0], down).wait_send()

    @pl.when(me == 1)
    def _():
        remote(dn_out.at[:, few], dn_in.at[:, few], dn_send, dn_recv.at[0, 0], down).wait_send()


def emit_kernel(layer_ref, slot_ref, layer_out, slot_out, layer, slots, sems):
    count = slots.shape[0]
    loads = [pltpu.make_async_copy(layer_ref, layer, sems.at[0])]
    stores = [pltpu.make_async_copy(layer, layer_out, sems.at[1])]
    for c in range(count):
        loads.append(pltpu.make_async_copy(slot_ref.at[c], slots.at[c], sems.at[2 + c]))
        stores.append(pltpu.make_async_copy(slots.at[c], slot_out.at[c], sems.at[2 + count + c]))
    for load in loads:
        load.start()
    for load, store in zip(loads, stores):
        load.wait()
        store.start()
    for store in stores:
        store.wait()


def emit(layer, slots):
    hbm = pl.BlockSpec(memory_space=pl.ANY)
    return pl.pallas_call(
        emit_kernel,
        out_shape=(jax.ShapeDtypeStruct(layer.shape, layer.dtype), jax.ShapeDtypeStruct(slots.shape, slots.dtype)),
        in_specs=[hbm, hbm],
        out_specs=(hbm, hbm),
        scratch_shapes=[pltpu.VMEM(layer.shape, layer.dtype), pltpu.VMEM(slots.shape, slots.dtype),
                        pltpu.SemaphoreType.DMA((2 + 2 * slots.shape[0],))],
        compiler_params=pltpu.CompilerParams(vmem_limit_bytes=60 << 20),
        name="emit",
    )(layer, slots)


def fused(starts, slots, q, k, v, f, rate, beta, gates, gain, weight):
    n = lax.axis_size("seq")
    nh = lax.axis_size("head")
    length, total = q.shape
    heads = beta.shape[1]
    width = total // heads
    half = length // 2
    depth, model = weight.shape
    piece = model // (2 * nh)
    owned = slots.shape[0] // n
    lanes = max(min(ENDS_MAX * (p + 1), owned * (n - 1 - p)) for p in range(n - 1))
    entries = owned + 2 * lanes
    hbm = pl.BlockSpec(memory_space=pl.ANY)
    dma = pltpu.SemaphoreType.DMA
    cube = pltpu.VMEM((heads, width, width), BF16)
    flow = pltpu.VMEM((heads, lanes, width, width), BF16)
    slab = pltpu.VMEM((length, total), BF16)
    return pl.pallas_call(
        functools.partial(fused_kernel, n, nh, lanes),
        out_shape=(jax.ShapeDtypeStruct((piece, length), BF16),
                   jax.ShapeDtypeStruct((owned, heads, width, width), BF16)),
        in_specs=[hbm] * 11,
        out_specs=(hbm, hbm),
        scratch_shapes=[
            pltpu.VMEM((piece, length), BF16), pltpu.VMEM((owned, heads, width, width), BF16),
            dma((heads // PAIR + 1,)),
            slab, slab, slab, slab, slab,
            pltpu.VMEM((1, total), F32),
            pltpu.VMEM((heads, length), BF16),
            pltpu.VMEM((1, width), F32),
            pltpu.VMEM((depth, model), BF16),
            pltpu.VMEM((2 * length, length), BF16),
            pltpu.VMEM((length, length), F32),
            pltpu.VMEM((length, length), F32),
            pltpu.VMEM((half, half), F32),
            pltpu.VMEM((length, width), F32),
            pltpu.VMEM((entries + 2, 16, length), BF16),
            pltpu.VMEM((heads, length), F32),
            pltpu.SMEM((entries + 2 * lanes * (1 + 2 * owned),), F32),
            pltpu.VMEM((heads, 2, half, half), F32),
            pltpu.VMEM((heads, half, 2 * half), BF16),
            pltpu.VMEM((heads, length, length), BF16),
            pltpu.VMEM((heads, length, 2 * width), BF16),
            pltpu.VMEM((heads, length, width), F32),
            pltpu.VMEM((heads, width, length), BF16),
            pltpu.VMEM((heads, 8, width), F32),
            pltpu.VMEM((heads, length, width), F32),
            pltpu.VMEM((heads, width + length, width), BF16),
            pltpu.VMEM((heads, width, width), F32),
            pltpu.VMEM((heads, owned, width, width), BF16),
            cube,
            slab,
            cube, cube,
            flow, flow, flow, flow,
            pltpu.VMEM((2 * nh, length, piece), BF16),
            pltpu.VMEM((nh, length, piece), BF16),
            pltpu.VMEM((nh, length, piece), BF16),
            pltpu.VMEM((nh, length, piece), BF16),
            pltpu.SMEM(starts.shape, I32), pltpu.SMEM(slots.shape, I32),
            dma((heads // PAIR, 4)), dma((7,)),
            dma, dma((heads,)), dma, dma((heads, lanes)), dma, dma((heads, lanes)),
            dma((nh,)), dma((nh,)), dma((nh,)), dma((nh,)),
        ],
        compiler_params=pltpu.CompilerParams(collective_id=0, has_side_effects=True,
                                             vmem_limit_bytes=60 << 20),
        name="fused",
    )(starts, slots, q, k, v, f, rate.reshape(1, -1), beta.T, gates, gain.reshape(1, -1), weight)


def per_device(query_proj, key_proj, value_proj, forget_logits, decay_rate, beta_logits,
               gate_logits, norm_gain, out_weight, stream_starts, stream_slots):
    layer, slots = fused(stream_starts, stream_slots, query_proj, key_proj, value_proj, forget_logits, decay_rate,
                 beta_logits, gate_logits, norm_gain, out_weight)
    layer, slots = emit(layer, slots)
    return layer.T, slots


def solution(mesh):
    rows = P(("groups", "seq"), ("head", "rep"))
    in_specs = (rows, rows, rows, rows, P(("head", "rep")), rows, rows, P(),
                P(("head", "rep"), None), P("groups"), P("groups"))
    out_specs = (rows, P(("groups", "seq"), ("head", "rep"), None, None))
    return jax.shard_map(per_device, mesh=mesh, in_specs=in_specs, out_specs=out_specs, check_vma=False)
```

```python
import functools
import jax
import jax.numpy as jnp
from jax import lax
from jax.experimental import pallas as pl
from jax.experimental.pallas import tpu as pltpu
from jax.sharding import PartitionSpec as P

ENDS_MAX = 4
PAIR = 2
BASE = 16
F32 = jnp.float32
BF16 = jnp.bfloat16
I32 = jnp.int32
NN = (((1,), (0,)), ((), ()))
NT = (((1,), (1,)), ((), ()))


def halves(x):
    high = x.astype(BF16)
    return high, (x - high.astype(F32)).astype(BF16)


def dot(a, b, dims=NN):
    return lax.dot_general(a, b, dims, preferred_element_type=F32)


def wide(x):
    return jnp.concatenate(halves(x), axis=1)


def twice(x, axis):
    return jnp.concatenate([x, x], axis=axis)


def mm4(a, b):
    both = dot(a, twice(b, 0))
    half = both.shape[1] // 2
    return both[:, :half] + both[:, half:]


def unit(x):
    return x * lax.rsqrt(jnp.sum(x * x, axis=-1, keepdims=True) + 1e-06)


def block_inverses(mats, level):
    size = mats[0].shape[0]
    row = lax.broadcasted_iota(I32, (size, size), 0)
    col = lax.broadcasted_iota(I32, (size, size), 1)
    eye = (row == col).astype(F32)
    powers = [jnp.where(level == 0.0, m, 0.0) for m in mats]
    result = [eye - p for p in powers]
    splits = [wide(p) for p in powers]
    powers = [mm4(s, s) for s in splits]
    yield None
    width = 4
    while width < BASE:
        splits = [wide(p) for p in powers]
        both = [mm4(jnp.concatenate([wide(r), s], axis=0), s) for r, s in zip(result, splits)]
        result = [r + b[:size] for r, b in zip(result, both)]
        powers = [b[size:] for b in both]
        width *= 2
        yield None
    splits = [wide(p) for p in powers]
    result = [r + mm4(wide(r), s) for r, s in zip(result, splits)]
    yield None
    width = BASE
    step = 1
    while width < size:
        splits = [r.astype(BF16) for r in result]
        mids = [dot(jnp.where(level == float(step), m, 0.0).astype(BF16), s) for m, s in zip(mats, splits)]
        yield None
        result = [r - dot(s, t.astype(BF16)) for r, s, t in zip(result, splits, mids)]
        width *= 2
        step += 1
        yield None
    yield result


def fused_kernel(n, nh, lanes, *refs):
    (starts_hbm, slots_hbm, q_hbm, k_hbm, v_hbm, f_hbm, rate_hbm, beta_hbm, gate_hbm, gain_hbm, weight_hbm,
     layer_hbm, slot_hbm,
     layer_ref, slot_ref, out_sem,
     qv, kv, vv, fv, gate, rate, beta_raw, gain, weight,
     sums, strict, lower, level, first, masks, betas, table,
     mat_s, link_s, reading_s, right_s, query_s, ended_s, keep_s,
     local, mapcorr, tail, own, moved, hidden, state_in, state_out,
     up_in, up_out, dn_in, dn_out, parts, pair_in, sums_out, cross_in,
     starts_ref, slots_ref, load_sem, misc_sem,
     st_send, st_recv, up_send, up_recv, dn_send, dn_recv, p_send, p_recv, c_send, c_recv) = refs
    length, total = qv.shape
    heads = own.shape[0]
    owned = own.shape[1]
    width = total // heads
    half = length // 2
    pairs = heads // PAIR
    streams = starts_ref.shape[0]
    piece = layer_ref.shape[0]
    me = lax.axis_index("seq")
    head_at = lax.axis_index("head")
    rep_at = lax.axis_index("rep")
    mesh_id = pl.DeviceIdType.MESH
    up, down, partner = {"seq": me + 1}, {"seq": me - 1}, {"rep": 1 - rep_at}
    has_up, has_down = me < n - 1, me > 0
    inner = has_up & has_down

    def pair_load(p, i):
        src, dst = ((f_hbm, fv), (k_hbm, kv), (q_hbm, qv), (v_hbm, vv))[i]
        cols = pl.ds(pl.multiple_of(p * PAIR * width, width), PAIR * width)
        return pltpu.make_async_copy(src.at[:, cols], dst.at[:, cols], load_sem.at[p, i])

    small = [pltpu.make_async_copy(src, dst, misc_sem.at[i]) for i, (src, dst) in enumerate(
        ((beta_hbm, beta_raw), (rate_hbm, rate), (gain_hbm, gain), (gate_hbm, gate), (weight_hbm, weight),
         (starts_hbm, starts_ref), (slots_hbm, slots_ref)))]
    for copy in small[5:] + small[:3]:
        copy.start()
    for p in range(pairs):
        for i in range(4):
            pair_load(p, i).start()
    for copy in small[3:5]:
        copy.start()

    barrier = pltpu.get_barrier_semaphore()

    @pl.when(has_up)
    def _():
        pl.semaphore_signal(barrier, inc=1, device_id=up, device_id_type=mesh_id)

    @pl.when(has_down)
    def _():
        pl.semaphore_signal(barrier, inc=1, device_id=down, device_id_type=mesh_id)

    pl.semaphore_signal(barrier, inc=1, device_id=partner, device_id_type=mesh_id)
    for j in range(1, nh):
        pl.semaphore_signal(barrier, inc=1, device_id={"head": lax.rem(head_at + j, nh)}, device_id_type=mesh_id)

    def remote(src, dst, send, recv, target):
        return pltpu.make_async_remote_copy(src_ref=src, dst_ref=dst, send_sem=send, recv_sem=recv,
                                            device_id=target, device_id_type=mesh_id)

    def state_copy(h):
        return remote(state_out.at[h], state_in.at[h], st_send, st_recv.at[h], up)

    def up_copy(h, c):
        return remote(up_out.at[h, c], up_in.at[h, c], up_send, up_recv.at[h, c], up)

    def dn_copy(h, c):
        return remote(dn_out.at[h, c], dn_in.at[h, c], dn_send, dn_recv.at[h, c], down)

    def pair_copy(j):
        return remote(parts.at[2 * j + 1 - rep_at], pair_in.at[j], p_send.at[j], p_recv.at[j], partner)

    def cross_copy(j):
        return remote(sums_out.at[j], cross_in.at[j], c_send.at[j], c_recv.at[j],
                      {"head": lax.rem(head_at + j, nh)})

    for copy in small[5:]:
        copy.wait()
    anchor = me * length
    begins = [starts_ref[j] for j in range(streams)]
    slots = [slots_ref[j] for j in range(streams)]
    ends = begins[1:] + [n * length]
    count = lambda flags: sum(f.astype(I32) for f in flags)
    where = jnp.where
    end_at = [count([e > p * length for p in range(1, n)]) if isinstance(e, jax.Array) else jnp.int32(n - 1)
              for e in ends]
    dest = [count([s >= p * owned for p in range(1, n)]) for s in slots]
    here = [e == me for e in end_at]
    before = where(me == 0, -1, count([b <= anchor - 1 for b in begins]))
    open_id = 1 + count([e <= me for e in end_at])
    open_flag = 1.0 - where(count(here) > 0, 1.0, 0.0)

    def colours(order, crossing, free, idle, late):
        busy = [jnp.int32(idle)] * lanes
        result = [None] * streams
        for j in order:
            left = crossing(j)
            last = left & late(j)
            left = left & jnp.logical_not(last)
            pick_at = where(last, lanes - 1, -1)
            for c in range(lanes):
                pick = left & free(busy[c], end_at[j])
                pick_at = where(pick, c, pick_at)
                left = left & jnp.logical_not(pick)
                if c == lanes - 1:
                    pick = pick | last
                busy[c] = where(pick, dest[j], busy[c])
            result[j] = pick_at
        return result

    up_lane = colours(list(range(streams)), lambda j: dest[j] > end_at[j], lambda b, e: b <= e, 0,
                      lambda j: jnp.bool_(False))
    dn_lane = colours(list(range(streams))[::-1], lambda j: dest[j] < end_at[j], lambda b, e: b >= e, n,
                      lambda j: (end_at[j] == n - 1) & (begins[j] < (n - 1) * length))
    code = []
    for j in range(streams):
        home = where(dest[j] == me, slots[j] - me * owned + 1, 0)
        rise = where(me == n - 2, slots[j] - (n - 1) * owned, up_lane[j]) + 1 + owned
        rise = where(dest[j] > me, rise, 0)
        fall = where(me == 1, slots[j], dn_lane[j]) + 1 + owned + lanes
        fall = where(dest[j] < me, fall, 0)
        code.append(where(here[j], home + rise + fall, 0))
    begun = sum(where(before == j + 1, code[j], 0) for j in range(streams))
    entries = owned + 2 * lanes
    for e in range(entries):
        table[e] = where(begun == e + 1, 1.0, 0.0)
    at = entries
    span = 1 + 2 * owned
    for lane_of, came, goes, far in ((up_lane, lambda j: end_at[j] < me, lambda j: dest[j] > me, n - 1),
                                     (dn_lane, lambda j: end_at[j] > me, lambda j: dest[j] < me, 0)):
        lane_in = [where(came(j), lane_of[j], -1) for j in range(streams)]
        passing = [where(goes(j), lane_in[j], -1) for j in range(streams)]
        places = [passing] + [[where(slots[j] == at_slot, lane_in[j], -1) for j in range(streams)]
                              for at_slot in [me * owned + k for k in range(owned)] + [far * owned + k for k in range(owned)]]
        for c in range(lanes):
            for x, lane_list in enumerate(places):
                table[at + x] = where(count([y == c for y in lane_list]) > 0, 1.0, 0.0)
            at += span
    up_base, dn_base = entries, entries + lanes * span

    pos_row = lax.broadcasted_iota(I32, (16, length), 1) + anchor
    pos_col = lax.broadcasted_iota(I32, (length, width), 0) + anchor
    seg_row = jnp.zeros((16, length), I32)
    seg_col = jnp.zeros((length, width), I32)
    for j in range(streams):
        seg_row = seg_row + where(pos_row >= begins[j], 1, 0)
        seg_col = seg_col + where(pos_col >= begins[j], 1, 0)
    code_row = jnp.zeros((16, length), I32)
    for j in range(streams):
        code_row = where(seg_row == j + 1, code[j], code_row)
    for e in range(entries):
        masks[e] = where(code_row == e + 1, 1.0, 0.0).astype(BF16)
    masks[entries] = where(seg_row == open_id, 1.0, 0.0).astype(BF16)
    first_row = where(seg_row == before, 1.0, 0.0)
    masks[entries + 1] = first_row.astype(BF16)
    any_first = jnp.max(first_row[:1])
    first[...] = where(seg_col == before, 1.0, 0.0)
    row = lax.broadcasted_iota(I32, (length, length), 0)
    col = lax.broadcasted_iota(I32, (length, length), 1)
    same = jnp.concatenate([seg_col] * (length // width), axis=1) == seg_row[:1]
    sums[:length] = where(row >= col, 1.0, 0.0).astype(BF16)
    sums[length:] = where(same & (col > row), 1.0, 0.0).astype(BF16)
    strict[...] = where(same & (row > col), 1.0, 0.0)
    lower[...] = where(same & (row >= col), 1.0, 0.0)
    hrow, hcol = row[:half, :half], col[:half, :half]
    depth = jnp.zeros((half, half), F32)
    size = BASE
    while size < half:
        depth = depth + where(hrow // size != hcol // size, 1.0, 0.0)
        size *= 2
    level[...] = depth

    small[0].wait()
    betas[...] = jax.nn.sigmoid(beta_raw[...].astype(F32))
    small[1].wait()

    @pl.when(me == 0)
    def _():
        for h in range(heads):
            state_in[h] = jnp.zeros((width, width), BF16)

    def prepare(p):
        for i in range(PAIR):
            h = p * PAIR + i
            cols = pl.ds(pl.multiple_of(h * width, width), width)
            q = unit(qv[:, cols].astype(F32))
            k = unit(kv[:, cols].astype(F32))
            yield None
            x = fv[:, cols].astype(F32)
            soft = jnp.maximum(x, 0.0) + jnp.log(1.0 + jnp.exp(-jnp.abs(x)))
            decay = -(rate[:, cols] * soft)
            summed = dot(sums[...], wide(decay))
            summed = summed[:, :width] + summed[:, width:]
            cum = summed[:length]
            yield None
            decayed = jnp.exp(cum) * first[...]
            beta = betas[pl.ds(h, 1), :]
            query_s[h] = q * decayed
            right_s[h] = jnp.concatenate([vv[:, cols], (k * decayed).astype(BF16)], axis=1)
            keep_s[h, :1] = jnp.exp(jnp.sum(first[...] * decay, axis=0, keepdims=True)) * any_first
            ended_s[h] = ((k * jnp.exp(summed[length:])).T * beta).astype(BF16)
            yield None
            cum0, cum1 = cum[:half], cum[half:]
            k0, k1, q0, q1 = k[:half], k[half:], q[:half], q[half:]
            mid0 = 0.5 * (cum0[:1] + cum0[-1:])
            mid1 = 0.5 * (cum1[:1] + cum1[-1:])
            up0, up1 = jnp.exp(cum0 - mid0), jnp.exp(cum1 - mid1)
            low0 = (k0 * jnp.exp(mid0 - cum0)).astype(BF16)
            low1 = jnp.concatenate([k0 * jnp.exp(mid1 - cum0), k1 * jnp.exp(mid1 - cum1)], axis=0).astype(BF16)
            block0 = dot(wide(jnp.concatenate([k0 * up0, q0 * up0], axis=0)), twice(low0, 1), NT)
            block1 = dot(wide(jnp.concatenate([k1 * up1, q1 * up1], axis=0)), twice(low1, 1), NT)
            yield None
            beta0, beta1 = beta[:, :half], beta[:, half:]
            mat_s[h, 0] = where(strict[:half, :half] > 0.0, block0[:half], 0.0) * beta0
            mat_s[h, 1] = where(strict[half:, half:] > 0.0, block1[:half, half:], 0.0) * beta1
            link_s[h] = wide(where(strict[half:, :half] > 0.0, block1[:half, :half], 0.0) * beta0)
            reading0 = where(lower[:half, :half] > 0.0, block0[half:], 0.0) * beta0
            reading1 = where(lower[half:, :] > 0.0, block1[half:], 0.0) * beta
            reading_s[h] = jnp.concatenate(
                [jnp.concatenate([reading0, jnp.zeros_like(reading0)], axis=1), reading1], axis=0).astype(BF16)
            yield None

    def local_pair(p, ahead):
        following = prepare(ahead)
        mats = [mat_s[p * PAIR + i, b] for i in range(PAIR) for b in range(2)]
        inverses = None
        for inverses in block_inverses(mats, level[...]):
            next(following, None)
        for _ in following:
            pass
        hr = lax.broadcasted_iota(I32, (width, width), 0)
        hc = lax.broadcasted_iota(I32, (width, width), 1)
        heads_of = [p * PAIR + i for i in range(PAIR)]
        right = [right_s[h] for h in heads_of]
        u0 = [dot(wide(inverses[2 * i]), twice(right[i][:half], 0)).astype(BF16) for i in range(PAIR)]
        rest = [right[i][half:].astype(F32) - dot(link_s[h], twice(u0[i], 0)) for i, h in enumerate(heads_of)]
        u1 = [dot(wide(inverses[2 * i + 1]), twice(rest[i].astype(BF16), 0)).astype(BF16) for i in range(PAIR)]
        for i, h in enumerate(heads_of):
            u = jnp.concatenate([u0[i], u1[i]], axis=0)
            chunks = ended_s[h].reshape(width // 16, 16, length)
            pick = lambda e: (chunks * masks[e][None]).reshape(width, length)
            states = dot(jnp.concatenate([pick(e) for e in range(entries + 1)], axis=0), u[:, :width])
            for c in range(owned):
                own[h, c] = states[c * width:(c + 1) * width].astype(BF16)
            for c in range(lanes):
                e = owned + c
                up_out[h, c] = states[e * width:(e + 1) * width].astype(BF16)
                e = owned + lanes + c
                dn_out[h, c] = states[e * width:(e + 1) * width].astype(BF16)
            tail[h] = states[entries * width:]
            through = dot(pick(entries + 1), u[:, width:])
            mapcorr[h, :width] = (where(hr == hc, keep_s[h, :1], 0.0) - through).astype(BF16)
            read = dot(reading_s[h], u)
            local[h] = read[:, :width]
            mapcorr[h, width:] = (query_s[h] - read[:, width:]).astype(BF16)

    def relay(p):
        for i in range(PAIR):
            h = p * PAIR + i

            @pl.when(has_down)
            def _():
                state_copy(h).wait_recv()

            applied = dot(mapcorr[h, :width], state_in[h])
            state_out[h] = (tail[h] + open_flag * applied).astype(BF16)

            @pl.when(has_up)
            def _():
                state_copy(h).start()

            moved[h] = applied.astype(BF16)

    def finish_heads(p):
        for i in range(PAIR):
            h = p * PAIR + i
            out = local[h] + dot(mapcorr[h, width:], state_in[h])
            cols = pl.ds(pl.multiple_of(h * width, width), width)
            scale = lax.rsqrt(jnp.mean(out * out, axis=-1, keepdims=True) + 1e-05)
            hidden[:, cols] = (out * scale * gain[...] * jax.nn.sigmoid(gate[:, cols].astype(F32))).astype(BF16)

    def chosen(terms):
        total = None
        for index, part in terms:
            factor = jnp.full((16, width), table[index], F32).astype(BF16)
            term = part.reshape(width // 16, 16, width) * factor[None]
            total = term if total is None else total + term
        return total.reshape(width, width)

    def shifted(own_part, entry, h, terms):
        value = own_part.astype(F32) + table[entry] * moved[h].astype(F32)
        if terms:
            value = value + chosen(terms).astype(F32)
        return value.astype(BF16)

    def up_flow(h):
        for c in range(lanes):
            up_copy(h, c).wait_recv()

            @pl.when(me < n - 2)
            def _():
                up_out[h, c] = shifted(up_out[h, c], owned + c, h, [(up_base + c * span, up_in[h, c])])
                up_copy(h, c).start()

        @pl.when(me == n - 2)
        def _():
            for k in range(owned):
                up_out[h, k] = shifted(up_out[h, k], owned + k, h,
                                       [(up_base + c * span + 1 + owned + k, up_in[h, c]) for c in range(lanes)])
                up_copy(h, k).start()

    def dn_lane_flow(h, c):
        @pl.when(me < n - 1)
        def _():
            dn_copy(h, c).wait_recv()
            dn_out[h, c] = shifted(dn_out[h, c], owned + lanes + c, h, [(dn_base + c * span, dn_in[h, c])])

        if c == lanes - 1:
            @pl.when(me == n - 1)
            def _():
                dn_out[h, c] = shifted(dn_out[h, c], owned + lanes + c, h, [])

        dn_copy(h, c).start()

    def dn_last_flow(h):
        for c in range(lanes):
            dn_copy(h, c).wait_recv()
        for k in range(owned):
            dn_out[h, k] = shifted(dn_out[h, k], owned + lanes + k, h,
                                   [(dn_base + c * span + 1 + owned + k, dn_in[h, c]) for c in range(lanes)])
            dn_copy(h, k).start()

    def store_layer():
        return pltpu.make_async_copy(layer_ref, layer_hbm, out_sem.at[pairs])

    def store_slots(p):
        some = pl.ds(p * PAIR, PAIR)
        return pltpu.make_async_copy(slot_ref.at[:, some], slot_hbm.at[:, some], out_sem.at[p])

    def settle(h):
        for k in range(owned):
            ups = [(up_base + c * span + 1 + k, up_in, c) for c in range(lanes)]
            downs = [(dn_base + c * span + 1 + k, dn_in, c) for c in range(lanes)]

            @pl.when(inner)
            def _():
                slot_ref[k, h] = shifted(own[h, k], k, h, [(x, ref[h, c]) for x, ref, c in ups + downs])

            @pl.when(me == 0)
            def _():
                dn_copy(h, k).wait_recv()
                slot_ref[k, h] = (own[h, k].astype(F32) + dn_in[h, k].astype(F32)).astype(BF16)

            @pl.when(me == n - 1)
            def _():
                up_copy(h, k).wait_recv()
                slot_ref[k, h] = (own[h, k].astype(F32) + table[k] * moved[h].astype(F32)
                                  + up_in[h, k].astype(F32)).astype(BF16)

    def project():
        if (2 * piece) % 128 == 0:
            for j in range(nh - 1, -1, -1):
                to = lax.rem(head_at + j, nh)
                cols = pl.ds(pl.multiple_of(to * 2 * piece, 128), 2 * piece)
                full = dot(hidden[...], weight[:, cols])
                parts[2 * to] = full[:, :piece].astype(BF16)
                parts[2 * to + 1] = full[:, piece:].astype(BF16)
                pair_copy(to).start()
        else:
            full = dot(hidden[...], weight[...])
            for d in range(2 * nh):
                parts[d] = full[:, d * piece:(d + 1) * piece].astype(BF16)
            for j in range(nh):
                pair_copy(j).start()

    def combine():
        for j in range(nh - 1, 0, -1):
            to = lax.rem(head_at + j, nh)
            pair_copy(to).wait_recv()
            sums_out[j] = (parts[2 * to + rep_at].astype(F32) + pair_in[to].astype(F32)).astype(BF16)
            cross_copy(j).start()
        pair_copy(head_at).wait_recv()

    def conclude():
        result = parts[2 * head_at + rep_at].astype(F32) + pair_in[head_at].astype(F32)
        for j in range(1, nh):
            cross_copy(j).wait_recv()
            result = result + cross_in[j].astype(F32)
        layer_ref[...] = result.T.astype(BF16)
        store_layer().start()

    below = n - 1 - me
    dn_last = 3 * n - 6
    settle_base = jnp.maximum(pairs + 1 + me, n - 1 + 2 * below)
    settle_base = where(me == 1, jnp.maximum(settle_base, dn_last + 1), settle_base)
    settle_base = where(me == n - 1, pairs + n, settle_base)
    settle_base = where(me == 0, dn_last + 2, settle_base)
    ticks = pairs + max(pairs + n, 3 * n - 5, dn_last + 2)

    def shifted_tick(x, extra):
        return where(x < pairs - 1, x, where(x < pairs - 1 + extra, -1, x - extra))

    def valid(x, limit):
        return (x >= 0) & (x < limit)

    def advance(t, carry):
        ahead = jnp.minimum(t + 1, pairs - 1)

        @pl.when(t + 1 < pairs)
        def _():
            for i in range(4):
                pair_load(ahead, i).wait()

        @pl.when(t < pairs)
        def _():
            local_pair(t, ahead)

        @pl.when((t == 0) & inner)
        def _():
            pl.semaphore_wait(barrier, nh + 2)

        @pl.when((t == 0) & jnp.logical_not(inner))
        def _():
            pl.semaphore_wait(barrier, nh + 1)

        p = t - me
        hu = t - me

        @pl.when(p == pairs)
        def _():
            combine()

        @pl.when(valid(p, pairs))
        def _():
            relay(p)

        @pl.when((me == 0) & (t < pairs))
        def _():
            for c in range(lanes):
                up_copy(t, c).start()

        @pl.when((me == 0) & (t == pairs - 1))
        def _():
            for h in range(pairs, heads):
                for c in range(lanes):
                    up_copy(h, c).start()

        @pl.when((me == n - 1) & (t < pairs))
        def _():
            for i in range(PAIR):
                for c in range(lanes - 1):
                    dn_copy(t * PAIR + i, c).start()

        @pl.when((me == n - 1) & valid(p, pairs))
        def _():
            for i in range(PAIR):
                dn_lane_flow(p * PAIR + i, lanes - 1)

        early = shifted_tick(t - (n - 4) - 2 * below, 0)

        @pl.when(inner & (me > 1) & valid(early, pairs))
        def _():
            for i in range(PAIR):
                for c in range(lanes - 1):
                    dn_lane_flow(early * PAIR + i, c)

        @pl.when(valid(p, pairs))
        def _():
            finish_heads(p)

        @pl.when(p == pairs - 1)
        def _():
            small[4].wait()
            project()

        @pl.when(inner & valid(hu, heads))
        def _():
            up_flow(hu)

        late = t - n + 2 - 2 * below - 0

        @pl.when(inner & (me > 1) & valid(late, pairs))
        def _():
            for i in range(PAIR):
                dn_lane_flow(late * PAIR + i, lanes - 1)

        last = shifted_tick(t - dn_last, 1)

        @pl.when((me == 1) & valid(last, pairs))
        def _():
            for i in range(PAIR):
                dn_last_flow(last * PAIR + i)

        @pl.when(t == where(me == 0, 9, where(me == n - 1, ticks - 2, ticks - 1)))
        def _():
            conclude()

        ps = t - settle_base

        @pl.when(valid(ps, pairs))
        def _():
            for i in range(PAIR):
                settle(ps * PAIR + i)
            store_slots(ps).start()

        return carry

    small[2].wait()
    small[3].wait()
    for i in range(4):
        pair_load(0, i).wait()
    for _ in prepare(0):
        pass
    lax.fori_loop(0, ticks, advance, 0)

    for j in range(nh):
        pair_copy(j).wait_send()
    for j in range(1, nh):
        cross_copy(j).wait_send()

    few = pl.ds(0, owned)
    store_layer().wait()
    for p in range(pairs):
        store_slots(p).wait()

    @pl.when(has_up)
    def _():
        remote(state_out, state_in, st_send, st_recv.at[0], up).wait_send()

    @pl.when(me < n - 2)
    def _():
        remote(up_out, up_in, up_send, up_recv.at[0, 0], up).wait_send()

    @pl.when(me == n - 2)
    def _():
        remote(up_out.at[:, few], up_in.at[:, few], up_send, up_recv.at[0, 0], up).wait_send()

    @pl.when(me > 1)
    def _():
        remote(dn_out, dn_in, dn_send, dn_recv.at[0, 0], down).wait_send()

    @pl.when(me == 1)
    def _():
        remote(dn_out.at[:, few], dn_in.at[:, few], dn_send, dn_recv.at[0, 0], down).wait_send()


def emit_kernel(layer_ref, slot_ref, layer_out, slot_out, layer, slots, sems):
    count = slots.shape[0]
    loads = [pltpu.make_async_copy(layer_ref, layer, sems.at[0])]
    stores = [pltpu.make_async_copy(layer, layer_out, sems.at[1])]
    for c in range(count):
        loads.append(pltpu.make_async_copy(slot_ref.at[c], slots.at[c], sems.at[2 + c]))
        stores.append(pltpu.make_async_copy(slots.at[c], slot_out.at[c], sems.at[2 + count + c]))
    for load in loads:
        load.start()
    for load, store in zip(loads, stores):
        load.wait()
        store.start()
    for store in stores:
        store.wait()


def emit(layer, slots):
    hbm = pl.BlockSpec(memory_space=pl.ANY)
    return pl.pallas_call(
        emit_kernel,
        out_shape=(jax.ShapeDtypeStruct(layer.shape, layer.dtype), jax.ShapeDtypeStruct(slots.shape, slots.dtype)),
        in_specs=[hbm, hbm],
        out_specs=(hbm, hbm),
        scratch_shapes=[pltpu.VMEM(layer.shape, layer.dtype), pltpu.VMEM(slots.shape, slots.dtype),
                        pltpu.SemaphoreType.DMA((2 + 2 * slots.shape[0],))],
        compiler_params=pltpu.CompilerParams(vmem_limit_bytes=60 << 20),
        name="emit",
    )(layer, slots)


def fused(starts, slots, q, k, v, f, rate, beta, gates, gain, weight):
    n = lax.axis_size("seq")
    nh = lax.axis_size("head")
    length, total = q.shape
    heads = beta.shape[1]
    width = total // heads
    half = length // 2
    depth, model = weight.shape
    piece = model // (2 * nh)
    owned = slots.shape[0] // n
    lanes = max(min(ENDS_MAX * (p + 1), owned * (n - 1 - p)) for p in range(n - 1))
    entries = owned + 2 * lanes
    hbm = pl.BlockSpec(memory_space=pl.ANY)
    dma = pltpu.SemaphoreType.DMA
    cube = pltpu.VMEM((heads, width, width), BF16)
    flow = pltpu.VMEM((heads, lanes, width, width), BF16)
    slab = pltpu.VMEM((length, total), BF16)
    return pl.pallas_call(
        functools.partial(fused_kernel, n, nh, lanes),
        out_shape=(jax.ShapeDtypeStruct((piece, length), BF16),
                   jax.ShapeDtypeStruct((owned, heads, width, width), BF16)),
        in_specs=[hbm] * 11,
        out_specs=(hbm, hbm),
        scratch_shapes=[
            pltpu.VMEM((piece, length), BF16), pltpu.VMEM((owned, heads, width, width), BF16),
            dma((heads // PAIR + 1,)),
            slab, slab, slab, slab, slab,
            pltpu.VMEM((1, total), F32),
            pltpu.VMEM((heads, length), BF16),
            pltpu.VMEM((1, width), F32),
            pltpu.VMEM((depth, model), BF16),
            pltpu.VMEM((2 * length, length), BF16),
            pltpu.VMEM((length, length), F32),
            pltpu.VMEM((length, length), F32),
            pltpu.VMEM((half, half), F32),
            pltpu.VMEM((length, width), F32),
            pltpu.VMEM((entries + 2, 16, length), BF16),
            pltpu.VMEM((heads, length), F32),
            pltpu.SMEM((entries + 2 * lanes * (1 + 2 * owned),), F32),
            pltpu.VMEM((heads, 2, half, half), F32),
            pltpu.VMEM((heads, half, 2 * half), BF16),
            pltpu.VMEM((heads, length, length), BF16),
            pltpu.VMEM((heads, length, 2 * width), BF16),
            pltpu.VMEM((heads, length, width), F32),
            pltpu.VMEM((heads, width, length), BF16),
            pltpu.VMEM((heads, 8, width), F32),
            pltpu.VMEM((heads, length, width), F32),
            pltpu.VMEM((heads, width + length, width), BF16),
            pltpu.VMEM((heads, width, width), F32),
            pltpu.VMEM((heads, owned, width, width), BF16),
            cube,
            slab,
            cube, cube,
            flow, flow, flow, flow,
            pltpu.VMEM((2 * nh, length, piece), BF16),
            pltpu.VMEM((nh, length, piece), BF16),
            pltpu.VMEM((nh, length, piece), BF16),
            pltpu.VMEM((nh, length, piece), BF16),
            pltpu.SMEM(starts.shape, I32), pltpu.SMEM(slots.shape, I32),
            dma((heads // PAIR, 4)), dma((7,)),
            dma, dma((heads,)), dma, dma((heads, lanes)), dma, dma((heads, lanes)),
            dma((nh,)), dma((nh,)), dma((nh,)), dma((nh,)),
        ],
        compiler_params=pltpu.CompilerParams(collective_id=0, has_side_effects=True,
                                             vmem_limit_bytes=60 << 20),
        name="fused",
    )(starts, slots, q, k, v, f, rate.reshape(1, -1), beta.T, gates, gain.reshape(1, -1), weight)


def per_device(query_proj, key_proj, value_proj, forget_logits, decay_rate, beta_logits,
               gate_logits, norm_gain, out_weight, stream_starts, stream_slots):
    layer, slots = fused(stream_starts, stream_slots, query_proj, key_proj, value_proj, forget_logits, decay_rate,
                 beta_logits, gate_logits, norm_gain, out_weight)
    layer, slots = emit(layer, slots)
    return layer.T, slots


def solution(mesh):
    rows = P(("groups", "seq"), ("head", "rep"))
    in_specs = (rows, rows, rows, rows, P(("head", "rep")), rows, rows, P(),
                P(("head", "rep"), None), P("groups"), P("groups"))
    out_specs = (rows, P(("groups", "seq"), ("head", "rep"), None, None))
    return jax.shard_map(per_device, mesh=mesh, in_specs=in_specs, out_specs=out_specs, check_vma=False)
```

```python
import functools
import jax
import jax.numpy as jnp
from jax import lax
from jax.experimental import pallas as pl
from jax.experimental.pallas import tpu as pltpu
from jax.sharding import PartitionSpec as P

ENDS_MAX = 4
PAIR = 2
BASE = 16
F32 = jnp.float32
BF16 = jnp.bfloat16
I32 = jnp.int32
NN = (((1,), (0,)), ((), ()))
NT = (((1,), (1,)), ((), ()))


def halves(x):
    high = x.astype(BF16)
    return high, (x - high.astype(F32)).astype(BF16)


def dot(a, b, dims=NN):
    return lax.dot_general(a, b, dims, preferred_element_type=F32)


def wide(x):
    return jnp.concatenate(halves(x), axis=1)


def twice(x, axis):
    return jnp.concatenate([x, x], axis=axis)


def mm4(a, b):
    both = dot(a, twice(b, 0))
    half = both.shape[1] // 2
    return both[:, :half] + both[:, half:]


def unit(x):
    return x * lax.rsqrt(jnp.sum(x * x, axis=-1, keepdims=True) + 1e-06)


def block_inverses(mats, level):
    size = mats[0].shape[0]
    row = lax.broadcasted_iota(I32, (size, size), 0)
    col = lax.broadcasted_iota(I32, (size, size), 1)
    eye = (row == col).astype(F32)
    powers = [jnp.where(level == 0.0, m, 0.0) for m in mats]
    result = [eye - p for p in powers]
    splits = [wide(p) for p in powers]
    powers = [mm4(s, s) for s in splits]
    yield None
    width = 4
    while width < BASE:
        splits = [wide(p) for p in powers]
        both = [mm4(jnp.concatenate([wide(r), s], axis=0), s) for r, s in zip(result, splits)]
        result = [r + b[:size] for r, b in zip(result, both)]
        powers = [b[size:] for b in both]
        width *= 2
        yield None
    splits = [wide(p) for p in powers]
    result = [r + mm4(wide(r), s) for r, s in zip(result, splits)]
    yield None
    width = BASE
    step = 1
    while width < size:
        splits = [r.astype(BF16) for r in result]
        mids = [dot(jnp.where(level == float(step), m, 0.0).astype(BF16), s) for m, s in zip(mats, splits)]
        yield None
        result = [r - dot(s, t.astype(BF16)) for r, s, t in zip(result, splits, mids)]
        width *= 2
        step += 1
        yield None
    yield result


def fused_kernel(n, nh, lanes, *refs):
    (starts_hbm, slots_hbm, q_hbm, k_hbm, v_hbm, f_hbm, rate_hbm, beta_hbm, gate_hbm, gain_hbm, weight_hbm,
     layer_hbm, slot_hbm,
     layer_ref, slot_ref, out_sem,
     qv, kv, vv, fv, gate, rate, beta_raw, gain, weight,
     sums, strict, lower, level, first, masks, betas, table,
     mat_s, link_s, reading_s, right_s, query_s, ended_s, keep_s,
     local, mapcorr, tail, own, moved, hidden, state_in, state_out,
     up_in, up_out, dn_in, dn_out, parts, pair_in, sums_out, cross_in,
     starts_ref, slots_ref, load_sem, misc_sem,
     st_send, st_recv, up_send, up_recv, dn_send, dn_recv, p_send, p_recv, c_send, c_recv) = refs
    length, total = qv.shape
    heads = own.shape[0]
    owned = own.shape[1]
    width = total // heads
    half = length // 2
    pairs = heads // PAIR
    streams = starts_ref.shape[0]
    piece = layer_ref.shape[0]
    me = lax.axis_index("seq")
    head_at = lax.axis_index("head")
    rep_at = lax.axis_index("rep")
    mesh_id = pl.DeviceIdType.MESH
    up, down, partner = {"seq": me + 1}, {"seq": me - 1}, {"rep": 1 - rep_at}
    has_up, has_down = me < n - 1, me > 0
    inner = has_up & has_down

    def pair_load(p, i):
        src, dst = ((f_hbm, fv), (k_hbm, kv), (q_hbm, qv), (v_hbm, vv))[i]
        cols = pl.ds(pl.multiple_of(p * PAIR * width, width), PAIR * width)
        return pltpu.make_async_copy(src.at[:, cols], dst.at[:, cols], load_sem.at[p, i])

    small = [pltpu.make_async_copy(src, dst, misc_sem.at[i]) for i, (src, dst) in enumerate(
        ((beta_hbm, beta_raw), (rate_hbm, rate), (gain_hbm, gain), (gate_hbm, gate), (weight_hbm, weight),
         (starts_hbm, starts_ref), (slots_hbm, slots_ref)))]
    for copy in small[5:] + small[:3]:
        copy.start()
    for p in range(pairs):
        for i in range(4):
            pair_load(p, i).start()
    for copy in small[3:5]:
        copy.start()

    barrier = pltpu.get_barrier_semaphore()

    @pl.when(has_up)
    def _():
        pl.semaphore_signal(barrier, inc=1, device_id=up, device_id_type=mesh_id)

    @pl.when(has_down)
    def _():
        pl.semaphore_signal(barrier, inc=1, device_id=down, device_id_type=mesh_id)

    pl.semaphore_signal(barrier, inc=1, device_id=partner, device_id_type=mesh_id)
    for j in range(1, nh):
        pl.semaphore_signal(barrier, inc=1, device_id={"head": lax.rem(head_at + j, nh)}, device_id_type=mesh_id)

    def remote(src, dst, send, recv, target):
        return pltpu.make_async_remote_copy(src_ref=src, dst_ref=dst, send_sem=send, recv_sem=recv,
                                            device_id=target, device_id_type=mesh_id)

    def state_copy(h):
        return remote(state_out.at[h], state_in.at[h], st_send, st_recv.at[h], up)

    def up_copy(h, c):
        return remote(up_out.at[h, c], up_in.at[h, c], up_send, up_recv.at[h, c], up)

    def dn_copy(h, c):
        return remote(dn_out.at[h, c], dn_in.at[h, c], dn_send, dn_recv.at[h, c], down)

    def pair_copy(j):
        return remote(parts.at[2 * j + 1 - rep_at], pair_in.at[j], p_send.at[j], p_recv.at[j], partner)

    def cross_copy(j):
        return remote(sums_out.at[j], cross_in.at[j], c_send.at[j], c_recv.at[j],
                      {"head": lax.rem(head_at + j, nh)})

    for copy in small[5:]:
        copy.wait()
    anchor = me * length
    begins = [starts_ref[j] for j in range(streams)]
    slots = [slots_ref[j] for j in range(streams)]
    ends = begins[1:] + [n * length]
    count = lambda flags: sum(f.astype(I32) for f in flags)
    where = jnp.where
    end_at = [count([e > p * length for p in range(1, n)]) if isinstance(e, jax.Array) else jnp.int32(n - 1)
              for e in ends]
    dest = [count([s >= p * owned for p in range(1, n)]) for s in slots]
    here = [e == me for e in end_at]
    before = where(me == 0, -1, count([b <= anchor - 1 for b in begins]))
    open_id = 1 + count([e <= me for e in end_at])
    open_flag = 1.0 - where(count(here) > 0, 1.0, 0.0)

    def colours(order, crossing, free, idle, late):
        busy = [jnp.int32(idle)] * lanes
        result = [None] * streams
        for j in order:
            left = crossing(j)
            last = left & late(j)
            left = left & jnp.logical_not(last)
            pick_at = where(last, lanes - 1, -1)
            for c in range(lanes):
                pick = left & free(busy[c], end_at[j])
                pick_at = where(pick, c, pick_at)
                left = left & jnp.logical_not(pick)
                if c == lanes - 1:
                    pick = pick | last
                busy[c] = where(pick, dest[j], busy[c])
            result[j] = pick_at
        return result

    up_lane = colours(list(range(streams)), lambda j: dest[j] > end_at[j], lambda b, e: b <= e, 0,
                      lambda j: jnp.bool_(False))
    dn_lane = colours(list(range(streams))[::-1], lambda j: dest[j] < end_at[j], lambda b, e: b >= e, n,
                      lambda j: (end_at[j] == n - 1) & (begins[j] < (n - 1) * length))
    code = []
    for j in range(streams):
        home = where(dest[j] == me, slots[j] - me * owned + 1, 0)
        rise = where(me == n - 2, slots[j] - (n - 1) * owned, up_lane[j]) + 1 + owned
        rise = where(dest[j] > me, rise, 0)
        fall = where(me == 1, slots[j], dn_lane[j]) + 1 + owned + lanes
        fall = where(dest[j] < me, fall, 0)
        code.append(where(here[j], home + rise + fall, 0))
    begun = sum(where(before == j + 1, code[j], 0) for j in range(streams))
    entries = owned + 2 * lanes
    for e in range(entries):
        table[e] = where(begun == e + 1, 1.0, 0.0)
    at = entries
    span = 1 + 2 * owned
    for lane_of, came, goes, far in ((up_lane, lambda j: end_at[j] < me, lambda j: dest[j] > me, n - 1),
                                     (dn_lane, lambda j: end_at[j] > me, lambda j: dest[j] < me, 0)):
        lane_in = [where(came(j), lane_of[j], -1) for j in range(streams)]
        passing = [where(goes(j), lane_in[j], -1) for j in range(streams)]
        places = [passing] + [[where(slots[j] == at_slot, lane_in[j], -1) for j in range(streams)]
                              for at_slot in [me * owned + k for k in range(owned)] + [far * owned + k for k in range(owned)]]
        for c in range(lanes):
            for x, lane_list in enumerate(places):
                table[at + x] = where(count([y == c for y in lane_list]) > 0, 1.0, 0.0)
            at += span
    up_base, dn_base = entries, entries + lanes * span

    pos_row = lax.broadcasted_iota(I32, (16, length), 1) + anchor
    pos_col = lax.broadcasted_iota(I32, (length, width), 0) + anchor
    seg_row = jnp.zeros((16, length), I32)
    seg_col = jnp.zeros((length, width), I32)
    for j in range(streams):
        seg_row = seg_row + where(pos_row >= begins[j], 1, 0)
        seg_col = seg_col + where(pos_col >= begins[j], 1, 0)
    code_row = jnp.zeros((16, length), I32)
    for j in range(streams):
        code_row = where(seg_row == j + 1, code[j], code_row)
    for e in range(entries):
        masks[e] = where(code_row == e + 1, 1.0, 0.0).astype(BF16)
    masks[entries] = where(seg_row == open_id, 1.0, 0.0).astype(BF16)
    first_row = where(seg_row == before, 1.0, 0.0)
    masks[entries + 1] = first_row.astype(BF16)
    any_first = jnp.max(first_row[:1])
    first[...] = where(seg_col == before, 1.0, 0.0)
    row = lax.broadcasted_iota(I32, (length, length), 0)
    col = lax.broadcasted_iota(I32, (length, length), 1)
    same = jnp.concatenate([seg_col] * (length // width), axis=1) == seg_row[:1]
    sums[:length] = where(row >= col, 1.0, 0.0).astype(BF16)
    sums[length:] = where(same & (col > row), 1.0, 0.0).astype(BF16)
    strict[...] = where(same & (row > col), 1.0, 0.0)
    lower[...] = where(same & (row >= col), 1.0, 0.0)
    hrow, hcol = row[:half, :half], col[:half, :half]
    depth = jnp.zeros((half, half), F32)
    size = BASE
    while size < half:
        depth = depth + where(hrow // size != hcol // size, 1.0, 0.0)
        size *= 2
    level[...] = depth

    small[0].wait()
    betas[...] = jax.nn.sigmoid(beta_raw[...].astype(F32))
    small[1].wait()

    @pl.when(me == 0)
    def _():
        for h in range(heads):
            state_in[h] = jnp.zeros((width, width), BF16)

    def prepare(p):
        for i in range(PAIR):
            h = p * PAIR + i
            cols = pl.ds(pl.multiple_of(h * width, width), width)
            q = unit(qv[:, cols].astype(F32))
            k = unit(kv[:, cols].astype(F32))
            yield None
            x = fv[:, cols].astype(F32)
            soft = jnp.maximum(x, 0.0) + jnp.log(1.0 + jnp.exp(-jnp.abs(x)))
            decay = -(rate[:, cols] * soft)
            summed = dot(sums[...], wide(decay))
            summed = summed[:, :width] + summed[:, width:]
            cum = summed[:length]
            yield None
            decayed = jnp.exp(cum) * first[...]
            beta = betas[pl.ds(h, 1), :]
            query_s[h] = q * decayed
            right_s[h] = jnp.concatenate([vv[:, cols], (k * decayed).astype(BF16)], axis=1)
            keep_s[h, :1] = jnp.exp(jnp.sum(first[...] * decay, axis=0, keepdims=True)) * any_first
            ended_s[h] = ((k * jnp.exp(summed[length:])).T * beta).astype(BF16)
            yield None
            cum0, cum1 = cum[:half], cum[half:]
            k0, k1, q0, q1 = k[:half], k[half:], q[:half], q[half:]
            mid0 = 0.5 * (cum0[:1] + cum0[-1:])
            mid1 = 0.5 * (cum1[:1] + cum1[-1:])
            up0, up1 = jnp.exp(cum0 - mid0), jnp.exp(cum1 - mid1)
            low0 = (k0 * jnp.exp(mid0 - cum0)).astype(BF16)
            low1 = jnp.concatenate([k0 * jnp.exp(mid1 - cum0), k1 * jnp.exp(mid1 - cum1)], axis=0).astype(BF16)
            block0 = dot(wide(jnp.concatenate([k0 * up0, q0 * up0], axis=0)), twice(low0, 1), NT)
            block1 = dot(wide(jnp.concatenate([k1 * up1, q1 * up1], axis=0)), twice(low1, 1), NT)
            yield None
            beta0, beta1 = beta[:, :half], beta[:, half:]
            mat_s[h, 0] = where(strict[:half, :half] > 0.0, block0[:half], 0.0) * beta0
            mat_s[h, 1] = where(strict[half:, half:] > 0.0, block1[:half, half:], 0.0) * beta1
            link_s[h] = wide(where(strict[half:, :half] > 0.0, block1[:half, :half], 0.0) * beta0)
            reading0 = where(lower[:half, :half] > 0.0, block0[half:], 0.0) * beta0
            reading1 = where(lower[half:, :] > 0.0, block1[half:], 0.0) * beta
            reading_s[h] = jnp.concatenate(
                [jnp.concatenate([reading0, jnp.zeros_like(reading0)], axis=1), reading1], axis=0).astype(BF16)
            yield None

    def local_pair(p, ahead):
        following = prepare(ahead)
        mats = [mat_s[p * PAIR + i, b] for i in range(PAIR) for b in range(2)]
        inverses = None
        for inverses in block_inverses(mats, level[...]):
            next(following, None)
        for _ in following:
            pass
        hr = lax.broadcasted_iota(I32, (width, width), 0)
        hc = lax.broadcasted_iota(I32, (width, width), 1)
        heads_of = [p * PAIR + i for i in range(PAIR)]
        right = [right_s[h] for h in heads_of]
        u0 = [dot(wide(inverses[2 * i]), twice(right[i][:half], 0)).astype(BF16) for i in range(PAIR)]
        rest = [right[i][half:].astype(F32) - dot(link_s[h], twice(u0[i], 0)) for i, h in enumerate(heads_of)]
        u1 = [dot(wide(inverses[2 * i + 1]), twice(rest[i].astype(BF16), 0)).astype(BF16) for i in range(PAIR)]
        for i, h in enumerate(heads_of):
            u = jnp.concatenate([u0[i], u1[i]], axis=0)
            chunks = ended_s[h].reshape(width // 16, 16, length)
            pick = lambda e: (chunks * masks[e][None]).reshape(width, length)
            states = dot(jnp.concatenate([pick(e) for e in range(entries + 1)], axis=0), u[:, :width])
            for c in range(owned):
                own[h, c] = states[c * width:(c + 1) * width].astype(BF16)
            for c in range(lanes):
                e = owned + c
                up_out[h, c] = states[e * width:(e + 1) * width].astype(BF16)
                e = owned + lanes + c
                dn_out[h, c] = states[e * width:(e + 1) * width].astype(BF16)
            tail[h] = states[entries * width:]
            through = dot(pick(entries + 1), u[:, width:])
            mapcorr[h, :width] = (where(hr == hc, keep_s[h, :1], 0.0) - through).astype(BF16)
            right_s[h] = u

    def read_pair(p):
        for i in range(PAIR):
            h = p * PAIR + i
            read = dot(reading_s[h], right_s[h])
            local[h] = read[:, :width]
            mapcorr[h, width:] = (query_s[h] - read[:, width:]).astype(BF16)

    def relay(p):
        for i in range(PAIR):
            h = p * PAIR + i

            @pl.when(has_down)
            def _():
                state_copy(h).wait_recv()

            applied = dot(mapcorr[h, :width], state_in[h])
            state_out[h] = (tail[h] + open_flag * applied).astype(BF16)

            @pl.when(has_up)
            def _():
                state_copy(h).start()

            moved[h] = applied.astype(BF16)

    def finish_heads(p):
        for i in range(PAIR):
            h = p * PAIR + i
            out = local[h] + dot(mapcorr[h, width:], state_in[h])
            cols = pl.ds(pl.multiple_of(h * width, width), width)
            scale = lax.rsqrt(jnp.mean(out * out, axis=-1, keepdims=True) + 1e-05)
            hidden[:, cols] = (out * scale * gain[...] * jax.nn.sigmoid(gate[:, cols].astype(F32))).astype(BF16)

    def chosen(terms):
        total = None
        for index, part in terms:
            factor = jnp.full((16, width), table[index], F32).astype(BF16)
            term = part.reshape(width // 16, 16, width) * factor[None]
            total = term if total is None else total + term
        return total.reshape(width, width)

    def shifted(own_part, entry, h, terms):
        value = own_part.astype(F32) + table[entry] * moved[h].astype(F32)
        if terms:
            value = value + chosen(terms).astype(F32)
        return value.astype(BF16)

    def up_flow(h):
        for c in range(lanes):
            up_copy(h, c).wait_recv()

            @pl.when(me < n - 2)
            def _():
                up_out[h, c] = shifted(up_out[h, c], owned + c, h, [(up_base + c * span, up_in[h, c])])
                up_copy(h, c).start()

        @pl.when(me == n - 2)
        def _():
            for k in range(owned):
                up_out[h, k] = shifted(up_out[h, k], owned + k, h,
                                       [(up_base + c * span + 1 + owned + k, up_in[h, c]) for c in range(lanes)])
                up_copy(h, k).start()

    def dn_lane_flow(h, c):
        @pl.when(me < n - 1)
        def _():
            dn_copy(h, c).wait_recv()
            dn_out[h, c] = shifted(dn_out[h, c], owned + lanes + c, h, [(dn_base + c * span, dn_in[h, c])])

        if c == lanes - 1:
            @pl.when(me == n - 1)
            def _():
                dn_out[h, c] = shifted(dn_out[h, c], owned + lanes + c, h, [])

        dn_copy(h, c).start()

    def dn_last_flow(h):
        for c in range(lanes):
            dn_copy(h, c).wait_recv()
        for k in range(owned):
            dn_out[h, k] = shifted(dn_out[h, k], owned + lanes + k, h,
                                   [(dn_base + c * span + 1 + owned + k, dn_in[h, c]) for c in range(lanes)])
            dn_copy(h, k).start()

    def store_layer():
        return pltpu.make_async_copy(layer_ref, layer_hbm, out_sem.at[pairs])

    def store_slots(p):
        some = pl.ds(p * PAIR, PAIR)
        return pltpu.make_async_copy(slot_ref.at[:, some], slot_hbm.at[:, some], out_sem.at[p])

    def settle(h):
        for k in range(owned):
            ups = [(up_base + c * span + 1 + k, up_in, c) for c in range(lanes)]
            downs = [(dn_base + c * span + 1 + k, dn_in, c) for c in range(lanes)]

            @pl.when(inner)
            def _():
                slot_ref[k, h] = shifted(own[h, k], k, h, [(x, ref[h, c]) for x, ref, c in ups + downs])

            @pl.when(me == 0)
            def _():
                dn_copy(h, k).wait_recv()
                slot_ref[k, h] = (own[h, k].astype(F32) + dn_in[h, k].astype(F32)).astype(BF16)

            @pl.when(me == n - 1)
            def _():
                up_copy(h, k).wait_recv()
                slot_ref[k, h] = (own[h, k].astype(F32) + table[k] * moved[h].astype(F32)
                                  + up_in[h, k].astype(F32)).astype(BF16)

    def project():
        if (2 * piece) % 128 == 0:
            for j in range(nh - 1, -1, -1):
                to = lax.rem(head_at + j, nh)
                cols = pl.ds(pl.multiple_of(to * 2 * piece, 128), 2 * piece)
                full = dot(hidden[...], weight[:, cols])
                parts[2 * to] = full[:, :piece].astype(BF16)
                parts[2 * to + 1] = full[:, piece:].astype(BF16)
                pair_copy(to).start()
        else:
            full = dot(hidden[...], weight[...])
            for d in range(2 * nh):
                parts[d] = full[:, d * piece:(d + 1) * piece].astype(BF16)
            for j in range(nh):
                pair_copy(j).start()

    def combine():
        for j in range(nh - 1, 0, -1):
            to = lax.rem(head_at + j, nh)
            pair_copy(to).wait_recv()
            sums_out[j] = (parts[2 * to + rep_at].astype(F32) + pair_in[to].astype(F32)).astype(BF16)
            cross_copy(j).start()
        pair_copy(head_at).wait_recv()

    def conclude():
        result = parts[2 * head_at + rep_at].astype(F32) + pair_in[head_at].astype(F32)
        for j in range(1, nh):
            cross_copy(j).wait_recv()
            result = result + cross_in[j].astype(F32)
        layer_ref[...] = result.T.astype(BF16)
        store_layer().start()

    below = n - 1 - me
    dn_last = 3 * n - 6
    settle_base = jnp.maximum(pairs + 1 + me, n - 1 + 2 * below)
    settle_base = where(me == 1, jnp.maximum(settle_base, dn_last + 1), settle_base)
    settle_base = where(me == n - 1, pairs + n, settle_base)
    settle_base = where(me == 0, dn_last + 2, settle_base)
    ticks = pairs + max(pairs + n, 3 * n - 5, dn_last + 2)

    def shifted_tick(x, extra):
        return where(x < pairs - 1, x, where(x < pairs - 1 + extra, -1, x - extra))

    def valid(x, limit):
        return (x >= 0) & (x < limit)

    def advance(t, carry):
        ahead = jnp.minimum(t + 1, pairs - 1)

        @pl.when(t + 1 < pairs)
        def _():
            for i in range(4):
                pair_load(ahead, i).wait()

        @pl.when(t < pairs)
        def _():
            local_pair(t, ahead)

        @pl.when((t == 0) & inner)
        def _():
            pl.semaphore_wait(barrier, nh + 2)

        @pl.when((t == 0) & jnp.logical_not(inner))
        def _():
            pl.semaphore_wait(barrier, nh + 1)

        p = t - me
        hu = t - me

        @pl.when(p == pairs)
        def _():
            combine()

        @pl.when(valid(p, pairs))
        def _():
            relay(p)

        @pl.when((me == 0) & (t < pairs))
        def _():
            for c in range(lanes):
                up_copy(t, c).start()

        @pl.when((me == 0) & (t == pairs - 1))
        def _():
            for h in range(pairs, heads):
                for c in range(lanes):
                    up_copy(h, c).start()

        @pl.when((me == n - 1) & (t < pairs))
        def _():
            for i in range(PAIR):
                for c in range(lanes - 1):
                    dn_copy(t * PAIR + i, c).start()

        @pl.when((me == n - 1) & valid(p, pairs))
        def _():
            for i in range(PAIR):
                dn_lane_flow(p * PAIR + i, lanes - 1)

        early = shifted_tick(t - (n - 4) - 2 * below, 0)

        @pl.when(inner & (me > 1) & valid(early, pairs))
        def _():
            for i in range(PAIR):
                for c in range(lanes - 1):
                    dn_lane_flow(early * PAIR + i, c)

        @pl.when(t < pairs)
        def _():
            read_pair(t)

        @pl.when(valid(p, pairs))
        def _():
            finish_heads(p)

        @pl.when(p == pairs - 1)
        def _():
            small[4].wait()
            project()

        @pl.when(inner & valid(hu, heads))
        def _():
            up_flow(hu)

        late = t - n + 2 - 2 * below - 0

        @pl.when(inner & (me > 1) & valid(late, pairs))
        def _():
            for i in range(PAIR):
                dn_lane_flow(late * PAIR + i, lanes - 1)

        last = shifted_tick(t - dn_last, 1)

        @pl.when((me == 1) & valid(last, pairs))
        def _():
            for i in range(PAIR):
                dn_last_flow(last * PAIR + i)

        @pl.when(t == where(me == 0, 9, where(me == n - 1, ticks - 2, ticks - 1)))
        def _():
            conclude()

        ps = t - settle_base

        @pl.when(valid(ps, pairs))
        def _():
            for i in range(PAIR):
                settle(ps * PAIR + i)
            store_slots(ps).start()

        return carry

    small[2].wait()
    small[3].wait()
    for i in range(4):
        pair_load(0, i).wait()
    for _ in prepare(0):
        pass
    lax.fori_loop(0, ticks, advance, 0)

    for j in range(nh):
        pair_copy(j).wait_send()
    for j in range(1, nh):
        cross_copy(j).wait_send()

    few = pl.ds(0, owned)
    store_layer().wait()
    for p in range(pairs):
        store_slots(p).wait()

    @pl.when(has_up)
    def _():
        remote(state_out, state_in, st_send, st_recv.at[0], up).wait_send()

    @pl.when(me < n - 2)
    def _():
        remote(up_out, up_in, up_send, up_recv.at[0, 0], up).wait_send()

    @pl.when(me == n - 2)
    def _():
        remote(up_out.at[:, few], up_in.at[:, few], up_send, up_recv.at[0, 0], up).wait_send()

    @pl.when(me > 1)
    def _():
        remote(dn_out, dn_in, dn_send, dn_recv.at[0, 0], down).wait_send()

    @pl.when(me == 1)
    def _():
        remote(dn_out.at[:, few], dn_in.at[:, few], dn_send, dn_recv.at[0, 0], down).wait_send()


def emit_kernel(layer_ref, slot_ref, layer_out, slot_out, layer, slots, sems):
    count = slots.shape[0]
    loads = [pltpu.make_async_copy(layer_ref, layer, sems.at[0])]
    stores = [pltpu.make_async_copy(layer, layer_out, sems.at[1])]
    for c in range(count):
        loads.append(pltpu.make_async_copy(slot_ref.at[c], slots.at[c], sems.at[2 + c]))
        stores.append(pltpu.make_async_copy(slots.at[c], slot_out.at[c], sems.at[2 + count + c]))
    for load in loads:
        load.start()
    for load, store in zip(loads, stores):
        load.wait()
        store.start()
    for store in stores:
        store.wait()


def emit(layer, slots):
    hbm = pl.BlockSpec(memory_space=pl.ANY)
    return pl.pallas_call(
        emit_kernel,
        out_shape=(jax.ShapeDtypeStruct(layer.shape, layer.dtype), jax.ShapeDtypeStruct(slots.shape, slots.dtype)),
        in_specs=[hbm, hbm],
        out_specs=(hbm, hbm),
        scratch_shapes=[pltpu.VMEM(layer.shape, layer.dtype), pltpu.VMEM(slots.shape, slots.dtype),
                        pltpu.SemaphoreType.DMA((2 + 2 * slots.shape[0],))],
        compiler_params=pltpu.CompilerParams(vmem_limit_bytes=60 << 20),
        name="emit",
    )(layer, slots)


def fused(starts, slots, q, k, v, f, rate, beta, gates, gain, weight):
    n = lax.axis_size("seq")
    nh = lax.axis_size("head")
    length, total = q.shape
    heads = beta.shape[1]
    width = total // heads
    half = length // 2
    depth, model = weight.shape
    piece = model // (2 * nh)
    owned = slots.shape[0] // n
    lanes = max(min(ENDS_MAX * (p + 1), owned * (n - 1 - p)) for p in range(n - 1))
    entries = owned + 2 * lanes
    hbm = pl.BlockSpec(memory_space=pl.ANY)
    dma = pltpu.SemaphoreType.DMA
    cube = pltpu.VMEM((heads, width, width), BF16)
    flow = pltpu.VMEM((heads, lanes, width, width), BF16)
    slab = pltpu.VMEM((length, total), BF16)
    return pl.pallas_call(
        functools.partial(fused_kernel, n, nh, lanes),
        out_shape=(jax.ShapeDtypeStruct((piece, length), BF16),
                   jax.ShapeDtypeStruct((owned, heads, width, width), BF16)),
        in_specs=[hbm] * 11,
        out_specs=(hbm, hbm),
        scratch_shapes=[
            pltpu.VMEM((piece, length), BF16), pltpu.VMEM((owned, heads, width, width), BF16),
            dma((heads // PAIR + 1,)),
            slab, slab, slab, slab, slab,
            pltpu.VMEM((1, total), F32),
            pltpu.VMEM((heads, length), BF16),
            pltpu.VMEM((1, width), F32),
            pltpu.VMEM((depth, model), BF16),
            pltpu.VMEM((2 * length, length), BF16),
            pltpu.VMEM((length, length), F32),
            pltpu.VMEM((length, length), F32),
            pltpu.VMEM((half, half), F32),
            pltpu.VMEM((length, width), F32),
            pltpu.VMEM((entries + 2, 16, length), BF16),
            pltpu.VMEM((heads, length), F32),
            pltpu.SMEM((entries + 2 * lanes * (1 + 2 * owned),), F32),
            pltpu.VMEM((heads, 2, half, half), F32),
            pltpu.VMEM((heads, half, 2 * half), BF16),
            pltpu.VMEM((heads, length, length), BF16),
            pltpu.VMEM((heads, length, 2 * width), BF16),
            pltpu.VMEM((heads, length, width), F32),
            pltpu.VMEM((heads, width, length), BF16),
            pltpu.VMEM((heads, 8, width), F32),
            pltpu.VMEM((heads, length, width), F32),
            pltpu.VMEM((heads, width + length, width), BF16),
            pltpu.VMEM((heads, width, width), F32),
            pltpu.VMEM((heads, owned, width, width), BF16),
            cube,
            slab,
            cube, cube,
            flow, flow, flow, flow,
            pltpu.VMEM((2 * nh, length, piece), BF16),
            pltpu.VMEM((nh, length, piece), BF16),
            pltpu.VMEM((nh, length, piece), BF16),
            pltpu.VMEM((nh, length, piece), BF16),
            pltpu.SMEM(starts.shape, I32), pltpu.SMEM(slots.shape, I32),
            dma((heads // PAIR, 4)), dma((7,)),
            dma, dma((heads,)), dma, dma((heads, lanes)), dma, dma((heads, lanes)),
            dma((nh,)), dma((nh,)), dma((nh,)), dma((nh,)),
        ],
        compiler_params=pltpu.CompilerParams(collective_id=0, has_side_effects=True,
                                             vmem_limit_bytes=60 << 20),
        name="fused",
    )(starts, slots, q, k, v, f, rate.reshape(1, -1), beta.T, gates, gain.reshape(1, -1), weight)


def per_device(query_proj, key_proj, value_proj, forget_logits, decay_rate, beta_logits,
               gate_logits, norm_gain, out_weight, stream_starts, stream_slots):
    layer, slots = fused(stream_starts, stream_slots, query_proj, key_proj, value_proj, forget_logits, decay_rate,
                 beta_logits, gate_logits, norm_gain, out_weight)
    layer, slots = emit(layer, slots)
    return layer.T, slots


def solution(mesh):
    rows = P(("groups", "seq"), ("head", "rep"))
    in_specs = (rows, rows, rows, rows, P(("head", "rep")), rows, rows, P(),
                P(("head", "rep"), None), P("groups"), P("groups"))
    out_specs = (rows, P(("groups", "seq"), ("head", "rep"), None, None))
    return jax.shard_map(per_device, mesh=mesh, in_specs=in_specs, out_specs=out_specs, check_vma=False)
```
